32 devices in a mesh: hist: 4 (over y, x), ent: 8 (over z, core).
Axes of the slice: x: 2, y: 2, z: 4, core: 2. Of those that a mesh axis runs over, the one named last changes fastest.
Arguments:
- states: bfloat16 [4, 2048, 512], P('hist', 'ent'), may hold values from -6 to 6
- w_neigh: bfloat16 [2, 256, 256], replicated, may hold values from -0.375 to 0.375
- w_self: bfloat16 [512, 512], replicated, may hold values from -0.25 to 0.25
- w_gate: bfloat16 [512, 512], replicated, may hold values from -0.25 to 0.25
- b_gate: float32 [512], replicated, may hold values from -4 to 4
- relation: bfloat16 [460, 512], replicated, may hold values from -6 to 6
- edge_src: int32 [4, 4096], P('hist', 'ent'), may hold values from 0 to 255
- edge_rel: int32 [4, 4096], P('hist', 'ent'), may hold values from 0 to 459
- edge_dst: int32 [4, 4096], P('hist', 'ent'), may hold values from 0 to 255
- send_counts: int32 [4, 64], P('hist', 'ent'), may hold values from 8 to 64, as said below
- query_ent: int32 [1024], P('ent'), may hold values from 0 to 255
- query_rel: int32 [1024], P('ent'), may hold values from 0 to 459
- query_grad: float32 [1024, 512], P('ent'), may hold values from -6 to 6
Outputs:
- grad_states: float32 [4, 2048, 512], P('hist', 'ent')
- grad_neigh: float32 [2, 256, 256], replicated
- grad_self: float32 [512, 512], replicated
- grad_gate: float32 [512, 512], replicated
- grad_bias: float32 [512], replicated
- grad_relation: float32 [460, 512], replicated
The draws below stay inside these ranges and needn't reach their ends.
Inputs may be any that keep to these rules, and one draw needn't show every extreme that they name: `send_counts`: slots at or beyond their bucket's count hold arbitrary ids and carry no edge. In every snapshot one target partition receives exactly 64 slots in use from every source partition; which one is drawn.
All inputs are finite; a program needn't handle non-finite values.
Results may differ from the reference program's by a relative error of at most 0.0053.
Values may be sent and summed in bfloat16 or wider, within the bound.
No kernel may reach another device: no remote copies, remote signals or barrier semaphores. Data moves between devices by JAX's collectives and lax.ppermute only.
A program may use at most 64 MiB of HBM per device.

```python
import math
import jax
import jax.numpy as jnp
import numpy as np
from jax import lax

D = 512
NREL = 460
BLOCKS = 2
ENT_DEV = 256
EDGE_DEV = 512
Q_DEV = 128
HIST = 4
HALF = 256
CAP = 64
ENTITIES = 2048
EDGES = 4096
QUERIES = 1024
N_ENT = 8


def draw_send_counts(key, part):
    base_key, hot_key = jax.random.split(jax.random.fold_in(key, 17))
    filled = jax.random.randint(base_key, (HIST, N_ENT, N_ENT), CAP // 8, CAP + 1)
    hot_dest = jax.random.randint(hot_key, (HIST, 1, 1), 0, N_ENT)
    dest_index = lax.broadcasted_iota(jnp.int32, (HIST, N_ENT, N_ENT), 2)
    return jnp.where(dest_index == hot_dest, CAP, filled).reshape(HIST, N_ENT * N_ENT).astype(jnp.int32)


def plant(entries, stream_key, low, high):
    longest = entries.shape.index(max(entries.shape))
    spots = []
    for shift in (0, 1):
        where = [jax.random.randint(jax.random.fold_in(stream_key, axis), (), 0, length) for axis, length in enumerate(entries.shape)]
        where[longest] = (where[longest] + shift) % entries.shape[longest]
        spots.append(tuple(where))
    return entries.at[spots[0]].set(low).at[spots[1]].set(high)


def levels(stream_key, dims, shards, smallest, top_value):
    def one(position, parts):
        heights = jax.random.uniform(jax.random.fold_in(jax.random.fold_in(stream_key, 6), position), (parts,), jnp.float32, smallest / len(shards), top_value / len(shards))
        return jnp.repeat(jnp.exp(heights), dims[position] // parts).reshape((-1,) + (1,) * (len(dims) - position - 1))

    level = one(*shards[0])
    for cut in shards[1:]:
        level = level * one(*cut)
    return level


def cumulative_ranks(count, skew):
    weights = [(1 << 20) // math.isqrt(grade ** skew) + 1 for grade in range(1, count + 1)]
    deviation = 1 + sum(weights) // (1 << 30)
    return np.cumsum(np.array([max(1, weight // deviation) for weight in weights]))


def skewed_ids(rng, shape, amount, skew):
    grid = cumulative_ranks(amount, skew)
    lot = jax.random.randint(jax.random.fold_in(rng, 1), shape, 0, int(grid[amount - 1]))
    standing = jnp.searchsorted(jnp.asarray(grid, jnp.int32), lot, side="right")
    return jax.random.permutation(jax.random.fold_in(rng, 2), amount)[standing].astype(jnp.int32)


def centred(key, dims, scale, reach, shards=(), kind=jnp.bfloat16):
    factor_of = levels(key, dims, shards, -0.22, 0.18) if shards else 1.0
    values = jax.random.normal(key, dims, jnp.float32) * scale * factor_of
    return jnp.minimum(jnp.maximum(values, -reach), reach).astype(kind)


def setup_inputs(seed: int = 0) -> dict:
    streams_of = jax.random.split(jax.random.key(seed), 14)
    states = centred(streams_of[0], (HIST, ENTITIES, D), 1.0, 6.0, ((0, 4), (1, 8)))
    w_neigh = centred(streams_of[1], (BLOCKS, HALF, HALF), HALF ** -0.5, 0.375)
    w_self = centred(streams_of[2], (D, D), D ** -0.5, 0.25)
    w_gate = centred(streams_of[3], (D, D), D ** -0.5, 0.25)
    b_gate = centred(streams_of[4], (D,), 1.0, 4.0, (), jnp.float32)
    relation = centred(streams_of[5], (NREL, D), 1.0, 6.0)
    edge_src = plant(jax.random.randint(streams_of[6], (HIST, EDGES), 0, ENT_DEV), jax.random.fold_in(streams_of[6], 1), 0, ENT_DEV - 1).astype(jnp.int32)
    edge_rel = plant(skewed_ids(streams_of[7], (HIST, EDGES), NREL, 2), jax.random.fold_in(streams_of[7], 3), 0, NREL - 1).astype(jnp.int32)
    edge_dst = plant(jax.random.randint(streams_of[8], (HIST, EDGES), 0, ENT_DEV), jax.random.fold_in(streams_of[8], 1), 0, ENT_DEV - 1).astype(jnp.int32)
    send_counts = draw_send_counts(jax.random.fold_in(streams_of[13], 71), 0)
    query_ent = plant(jax.random.randint(streams_of[10], (QUERIES,), 0, ENT_DEV), jax.random.fold_in(streams_of[10], 1), 0, ENT_DEV - 1).astype(jnp.int32)
    query_rel = plant(skewed_ids(streams_of[11], (QUERIES,), NREL, 2), jax.random.fold_in(streams_of[11], 3), 0, NREL - 1).astype(jnp.int32)
    query_grad = centred(streams_of[12], (QUERIES, D), 1.0, 6.0, ((0, 8),), jnp.float32)
    return {"states": states, "w_neigh": w_neigh, "w_self": w_self, "w_gate": w_gate, "b_gate": b_gate, "relation": relation, "edge_src": edge_src, "edge_rel": edge_rel, "edge_dst": edge_dst, "send_counts": send_counts, "query_ent": query_ent, "query_rel": query_rel, "query_grad": query_grad}


def snapshot(hidden, cotangent, src_glob, rel_ids, dst_glob, in_use, w_neigh, w_self, w_gate, b_gate, relation):
    entities = hidden.shape[0]
    features = hidden.shape[1]
    blocks = w_neigh.shape[0]
    block_width = w_neigh.shape[1]
    edges_all = src_glob.shape[0]
    inputs = (hidden[src_glob].astype(jnp.float32) + relation[rel_ids].astype(jnp.float32)).astype(jnp.bfloat16)
    product = jnp.einsum('ebi,bij->ebj', inputs.reshape(edges_all, blocks, block_width).astype(jnp.float32), w_neigh.astype(jnp.float32))
    message = (product.reshape(edges_all, features) * in_use[:, None]).astype(jnp.bfloat16)
    indegree = jax.ops.segment_sum(in_use, dst_glob, num_segments=entities)
    scaling = 1.0 / jnp.maximum(indegree, 1.0)
    summed = jax.ops.segment_sum(message.astype(jnp.float32), dst_glob, num_segments=entities)
    pre_act = summed * scaling[:, None] + jnp.dot(hidden, w_self, preferred_element_type=jnp.float32)
    gate_open = jax.nn.sigmoid(jnp.dot(hidden, w_gate, preferred_element_type=jnp.float32) + b_gate)
    sigmoid_pre = jax.nn.sigmoid(pre_act)
    new_state = pre_act * sigmoid_pre
    keep_part = cotangent * (1.0 - gate_open)
    gate_term = cotangent * (new_state - hidden.astype(jnp.float32)) * gate_open * (1.0 - gate_open)
    gate_low = gate_term.astype(jnp.bfloat16)
    pre_term = cotangent * gate_open * (sigmoid_pre * (1.0 + pre_act * (1.0 - sigmoid_pre)))
    pre_low = pre_term.astype(jnp.bfloat16)
    grad_gate = jnp.dot(hidden.T, gate_low, preferred_element_type=jnp.float32)
    grad_bias = lax.optimization_barrier(jnp.sum(gate_term, axis=0))
    grad_self = jnp.dot(hidden.T, pre_low, preferred_element_type=jnp.float32)
    back_sum = keep_part + jnp.dot(gate_low, w_gate.T, preferred_element_type=jnp.float32)
    back_sum = back_sum + jnp.dot(pre_low, w_self.T, preferred_element_type=jnp.float32)
    replies = (pre_term[dst_glob] * scaling[dst_glob][:, None] * in_use[:, None]).astype(jnp.bfloat16)
    grad_neigh = jnp.einsum('ebi,ebj->bij', inputs.reshape(edges_all, blocks, block_width).astype(jnp.float32), replies.reshape(edges_all, blocks, block_width).astype(jnp.float32))
    spread = jnp.einsum('ebj,bij->ebi', replies.reshape(edges_all, blocks, block_width).astype(jnp.float32), w_neigh.astype(jnp.float32)).reshape(edges_all, features)
    back_sum = back_sum + jax.ops.segment_sum(spread, src_glob, num_segments=entities)
    grad_rel = jax.ops.segment_sum(spread, rel_ids, num_segments=relation.shape[0])
    return (back_sum, (grad_neigh, grad_self, grad_gate, grad_bias, grad_rel))

def reference(states, w_neigh, w_self, w_gate, b_gate, relation, edge_src, edge_rel, edge_dst, send_counts, query_ent, query_rel, query_grad):
    edge_pos = jnp.arange(EDGES, dtype=jnp.int32)
    part_of = edge_pos // EDGE_DEV
    bucket = edge_pos % EDGE_DEV // CAP
    within = edge_pos % CAP
    owners = jnp.arange(QUERIES, dtype=jnp.int32) // Q_DEV
    rows_glob = (owners * ENT_DEV + query_ent).astype(jnp.int32)
    top_grad = jnp.zeros((ENTITIES, D), jnp.float32).at[rows_glob].add(query_grad.astype(jnp.float32))
    cotangent = top_grad
    totals = None
    collected = []
    for step_index in range(HIST - 1, -1, -1):
        counts = send_counts[step_index][(part_of * N_ENT + bucket).astype(jnp.int32)]
        in_use = (within < counts).astype(jnp.float32)
        src_glob = (part_of * ENT_DEV + edge_src[step_index]).astype(jnp.int32)
        dst_glob = (bucket * ENT_DEV + edge_dst[step_index]).astype(jnp.int32)
        back_sum, grads = snapshot(states[step_index], cotangent, src_glob, edge_rel[step_index], dst_glob, in_use, w_neigh, w_self, w_gate, b_gate, relation)
        if totals is None:
            totals = grads
        else:
            totals = tuple((a + b for a, b in zip(totals, grads)))
        collected.append(back_sum)
        cotangent = back_sum
    grad_states = jnp.stack(collected[::-1], axis=0)
    grad_neigh, grad_self, grad_gate, grad_bias, grad_rel = totals
    grad_rel = grad_rel + jax.ops.segment_sum(query_grad.astype(jnp.float32), query_rel, num_segments=NREL)
    factor = 1.0 / jnp.sqrt(jnp.float32(HIST * ENTITIES))
    return (grad_states, grad_neigh * factor, grad_self * factor, grad_gate * factor, grad_bias * factor, grad_rel * factor)
```

```python
import functools
import math

import jax
import jax.numpy as jnp
from jax import lax
from jax.experimental import pallas as pl
from jax.experimental.pallas import tpu as pltpu
from jax.sharding import PartitionSpec as P

BF = jnp.bfloat16
F32 = jnp.float32
TALL = (((0,), (0,)), ((), ()))
WIDE = (((1,), (1,)), ((), ()))
LANES = 128


def dot(a, b, dims=(((1,), (0,)), ((), ()))):
    return lax.dot_general(a, b, dims, preferred_element_type=F32)


def onehot(ids, rows):
    spot = lax.broadcasted_iota(jnp.int32, (rows, ids.shape[1]), 0)
    return jnp.where(spot == ids, 1.0, 0.0).astype(BF)


def round_up(value, step):
    return -(-value // step) * step


def block(shape, lead=None):
    if lead is None:
        return pl.BlockSpec(shape, lambda i: (0,) * len(shape))
    return pl.BlockSpec((None,) + shape, lambda i: (lead,) + (0,) * len(shape))


def whole(x):
    return block(x.shape)


def run(body, name, ins, specs, outs, scratch=()):
    return pl.pallas_call(
        body,
        name=name,
        grid=(1,),
        in_specs=specs,
        out_specs=[block(s.shape) for s in outs],
        out_shape=outs,
        scratch_shapes=list(scratch),
    )(*ins)


def sds(shape, dtype):
    return jax.ShapeDtypeStruct(shape, dtype)


def send_kernel(sections, groups, x, rel, src, dst, rid, counts, wn, msg, xp):
    ent_rows, features = x.shape
    slots = src.shape[1]
    room = slots // groups
    width = features // sections
    half = wn.shape[1]
    e = lax.axis_index("ent")
    ids = src[...]
    rids = rid[...]
    xv = x[...]
    got = dot(onehot(ids, ent_rows), xv, TALL) + dot(onehot(rids, rel.shape[0]), rel[...], TALL)
    inputs = got.astype(BF)
    for b in range(wn.shape[0]):
        out = dot(inputs[:, b * half : (b + 1) * half], wn[b]).astype(BF)
        for part in range(half // width):
            target = b * (half // width) + part
            for u in range(groups):
                msg[target * groups + u, :room, :] = out[
                    u * room : (u + 1) * room, part * width : (part + 1) * width
                ]
    lane = lax.broadcasted_iota(jnp.int32, (1, slots), 1)
    limit = jnp.zeros((1, slots), jnp.int32)
    for u in range(groups):
        limit = jnp.where(lane // room == u, counts[0, u], limit)
    live = jnp.where(lane % room < limit, dst[...], -1).astype(F32)
    per = width // room
    seat = lax.broadcasted_iota(jnp.int32, (8, width), 1) // room
    for u in range(groups):
        start = u * room // width * width
        row = jnp.broadcast_to(live[:, start : start + width], (8, width))
        turn = lax.rem(e - u + per * groups, per) * room
        row = pltpu.roll(row, turn, 1)
        row = jnp.where(seat == lax.rem(e, per), row, -1.0).astype(BF)
        for target in range(sections):
            msg[target * groups + u, room:, :] = row
    lines = slots // features
    extra = jnp.zeros((8, features), F32)
    level = lax.broadcasted_iota(jnp.int32, (8, features), 0)
    for k in range(lines):
        cut = slice(k * features, (k + 1) * features)
        for j, piece in enumerate((ids[:, cut], rids[:, cut] // 256, rids[:, cut] % 256)):
            extra = jnp.where(level == 3 * k + j, piece.astype(F32), extra)
    for target in range(sections):
        xp[target, :ent_rows, :] = xv
        xp[target, ent_rows:, :] = extra.astype(BF)


def state_kernel(recv, xp, wg, ws, bias, al, be, ka, sc, odt, osr, rid):
    groups = recv.shape[0]
    width = recv.shape[2]
    room = recv.shape[1] - 8
    features = xp.shape[1]
    ent_rows = xp.shape[0] - 8
    slots = groups * room
    per = width // room
    h = lax.axis_index("hist")
    cols = pl.ds(pl.multiple_of(h * width, width), width)
    summed = jnp.zeros((ent_rows, width), F32)
    degree = jnp.zeros((ent_rows, width), F32)
    ones = jnp.ones((width, width), BF)
    for g in range(groups // per):
        ids = recv[g * per, room:, :].astype(F32)
        for j in range(1, per):
            ids = jnp.maximum(ids, recv[g * per + j, room:, :].astype(F32))
        hot = onehot(ids[:1].astype(jnp.int32), ent_rows)
        rows = jnp.concatenate([recv[g * per + j, :room, :] for j in range(per)], axis=0)
        summed = summed + dot(hot, rows)
        degree = degree + dot(hot, ones)
        odt[g * width : (g + 1) * width, :] = hot.astype(F32).T.astype(BF)
    scaling = 1.0 / jnp.maximum(degree, 1.0)
    x = xp[:ent_rows, :]
    pre_act = summed * scaling + dot(x, ws[:, cols])
    gate_open = jax.nn.sigmoid(dot(x, wg[:, cols]) + bias[:, cols])
    sig = jax.nn.sigmoid(pre_act)
    new_state = pre_act * sig
    ka[...] = 1.0 - gate_open
    al[...] = (new_state - xp[:ent_rows, cols].astype(F32)) * gate_open * (1.0 - gate_open)
    be[...] = gate_open * (sig * (1.0 + pre_act * (1.0 - sig)))
    sc[...] = scaling
    extra = xp[ent_rows:, :].astype(F32).astype(jnp.int32)
    for k in range(slots // features):
        cut = slice(k * features, (k + 1) * features)
        osr[:, cut] = onehot(extra[3 * k : 3 * k + 1], ent_rows)
        ids = extra[3 * k + 1 : 3 * k + 2] * 256 + extra[3 * k + 2 : 3 * k + 3]
        rid[:, cut] = jnp.broadcast_to(ids, (8, features))


def query_kernel(qe, qr, qg, top, qp):
    width = top.shape[1]
    h = lax.axis_index("hist")
    cols = pl.ds(pl.multiple_of(h * width, width), width)
    grad = qg[:, cols]
    for ids, out in ((qe, top), (qr, qp)):
        hot = onehot(ids[...], out.shape[0]).astype(F32)
        out[...] = lax.dot_general(
            hot,
            grad,
            (((1,), (0,)), ((), ())),
            precision=lax.Precision.HIGHEST,
            preferred_element_type=F32,
        )


def top_kernel(count, *refs):
    parts = refs[:count]
    al, be, ka, sc, odt, c_out, gp, keep, bias, rep = refs[count:]
    width = al.shape[1]
    c = parts[0][...]
    for p in parts[1:]:
        c = c + p[...].astype(F32)
    gate_term = c * al[...]
    pre_term = c * be[...]
    rep[...] = dot(odt[...], (pre_term * sc[...]).astype(BF)).astype(BF)
    gp[:, :width] = gate_term.astype(BF)
    gp[:, width:] = pre_term.astype(BF)
    keep[...] = c * ka[...]
    c_out[...] = c
    bias[...] = jnp.broadcast_to(jnp.sum(gate_term, axis=0, keepdims=True), bias.shape)


def back_kernel(sections, ret, gp, osr, keep, wg, ws, wn, base, sp, *sends):
    width = keep.shape[1]
    half = wn.shape[1]
    h = lax.axis_index("hist")
    mine = pl.ds(pl.multiple_of(h * width, width), width)
    mine_in = pl.ds(pl.multiple_of(lax.rem(h * width, half), width), width)
    own = h * width // half
    s = dot(osr[...], ret[...])
    high = s.astype(BF)
    low = (s - high.astype(F32)).astype(BF)
    sp[:, :width] = high
    sp[:, width:] = low
    left = jnp.concatenate([gp[...], high, low], axis=1)
    for k in range(sections):
        to = lax.rem(h + k, sections)
        rows = pl.ds(pl.multiple_of(to * width, width), width)
        rows_in = pl.ds(pl.multiple_of(lax.rem(to * width, half), width), width)
        match = jnp.where(to * width // half == own, 1.0, 0.0).astype(BF)
        w = wn[own, rows_in, mine_in] * match
        right = jnp.concatenate([wg[rows, mine], ws[rows, mine], w, w], axis=1)
        out = dot(left, right, WIDE)
        if k == 0:
            base[...] = keep[...] + out
        else:
            sends[k - 1][...] = out.astype(BF)


def grad_kernel(half, first, xp, gp, sp, ret, rid, bias, *refs):
    ent_rows = gp.shape[0]
    width = sp.shape[1] // 2
    if first:
        gs_in = ns_in = r_in = b_in = None
        gs, ns, rs, bs = refs
    else:
        gs_in, ns_in, r_in, b_in, gs, ns, rs, bs = refs
    h = lax.axis_index("hist")
    own = h * width // half

    def put(out, before, value):
        out[...] = value if before is None else before[...] + value

    put(gs, gs_in, dot(xp[:ent_rows, :], gp[...], TALL))
    xb = xp[:ent_rows, pl.ds(pl.multiple_of(own * half, half), half)]
    both = dot(xb, sp[...], TALL)
    put(ns, ns_in, both[:, :width] + both[:, width:])
    put(rs, r_in, dot(onehot(rid[:1, :], rs.shape[0]), ret[...]))
    put(bs, b_in, bias[...])


def pack_kernel(sizes, gs, ns, rs, qp, bs, out):
    groups = out.shape[0]
    width = out.shape[2]
    pieces = (gs[:, :width], gs[:, width:], ns[...], rs[...], qp[...])
    for u in range(groups):
        at = 0
        for piece, size in zip(pieces, sizes):
            low = min(u * size, piece.shape[0])
            high = min(low + size, piece.shape[0])
            if high > low:
                out[u, at : at + high - low, :] = piece[low:high].astype(BF)
            if high - low < size:
                out[u, at + high - low : at + size, :] = jnp.zeros((size - high + low, width), BF)
            at += size
        out[u, at:, :] = jnp.concatenate([bs[...], bs[...]], axis=0).astype(BF)


def add_kernel(x, out):
    total = x[0].astype(F32)
    for u in range(1, x.shape[0]):
        total = total + x[u].astype(F32)
    for k in range(out.shape[0]):
        out[k] = total.astype(BF)


def last_kernel(sections, groups, sizes, factor, *refs):
    mine = refs[:sections]
    other = refs[sections]
    wn, rel, neigh, self_, gate, bias, relation, r_all, q_all, n_all = refs[sections + 1 :]
    width = mine[0].shape[2]
    blocks, half = wn.shape[0], wn.shape[1]
    relations = rel.shape[0]
    h = lax.axis_index("hist")
    core = lax.rem(lax.axis_index("ent"), 2)
    pairs = groups // 2
    for k in range(sections):
        to = lax.rem(h - k + sections, sections)
        cols = pl.ds(pl.multiple_of(to * width, width), width)
        for z in range(pairs):
            for flip in range(2):
                u = 2 * z + (core if flip == 0 else 1 - core)
                piece = mine[k].at[z] if flip == 0 else other.at[k * pairs + z]
                at = 0
                for out, size, scale in zip(
                    (gate, self_, n_all, r_all, q_all), sizes, (factor, factor, 1.0, 1.0, 1.0)
                ):
                    if True:
                        value = piece[at : at + size, :].astype(F32) * scale
                        where = pl.ds(pl.multiple_of(u * size, size), size)
                        out[where, cols] = value.astype(out.dtype)
                    at += size
        bias[:, cols] = mine[k][0, at : at + 8, :].astype(F32) * factor
    for b in range(blocks):
        cut = slice(b * half, (b + 1) * half)
        r = r_all[:relations, cut]
        neigh[b] = (n_all[:half, cut] + dot(rel[:, cut], r, TALL)) * factor
        relation[:, cut] = (q_all[:relations, cut] + dot(r, wn[b], WIDE)) * factor


def on_device(
    states,
    w_neigh,
    w_self,
    w_gate,
    b_gate,
    relation,
    edge_src,
    edge_rel,
    edge_dst,
    send_counts,
    query_ent,
    query_rel,
    query_grad,
):
    groups = lax.axis_size("ent")
    sections = lax.axis_size("hist")
    ent_rows, features = states.shape[1:]
    slots = edge_src.shape[1]
    room = slots // groups
    width = features // sections
    half = w_neigh.shape[1]
    relations = relation.shape[0]
    hidden = states[0]
    bias_row = b_gate.reshape(1, features)
    smem = pl.BlockSpec(memory_space=pltpu.SMEM)

    def a2a(x, axes):
        return lax.all_to_all(x, axes, split_axis=0, concat_axis=0, tiled=True)

    msg, xp = run(
        functools.partial(send_kernel, sections, groups),
        "send",
        (hidden, relation, edge_src, edge_dst, edge_rel, send_counts, w_neigh),
        [whole(hidden), whole(relation)] + [whole(edge_src)] * 3 + [smem, whole(w_neigh)],
        [
            sds((sections * groups, room + 8, width), BF),
            sds((sections, ent_rows + 8, features), BF),
        ],
    )
    recv = a2a(msg, ("hist", "ent")).reshape(sections, groups, room + 8, width)
    xg = a2a(xp, "hist")

    sizes = tuple(
        round_up(-(-rows // groups), 16) for rows in (features, features, half, relations, relations)
    )
    rel_rows = round_up(relations, 8)
    qe = query_ent.reshape(1, -1)
    qr = query_rel.reshape(1, -1)
    top, qp = run(
        query_kernel,
        "query",
        (qe, qr, query_grad),
        [whole(qe), whole(qr), whole(query_grad)],
        [sds((ent_rows, width), F32), sds((rel_rows, width), F32)],
    )

    def prepare(t):
        return run(
            state_kernel,
            "state",
            (recv, xg, w_gate, w_self, bias_row),
            [
                block(recv.shape[1:], t),
                block(xg.shape[1:], t),
                whole(w_gate),
                whole(w_self),
                whole(bias_row),
            ],
            [sds((ent_rows, width), F32)] * 4
            + [sds((slots, ent_rows), BF), sds((ent_rows, slots), BF), sds((8, slots), jnp.int32)],
        )

    parts = (top,)
    totals = None
    collected = [None] * sections
    for t in range(sections - 1, -1, -1):
        al, be, ka, sc, odt, osr, rid = prepare(t)
        ins = (*parts, al, be, ka, sc, odt)
        c, gp, keep, bias, rep = run(
            functools.partial(top_kernel, len(parts)),
            "top",
            ins,
            [whole(x) for x in ins],
            [
                sds((ent_rows, width), F32),
                sds((ent_rows, 2 * width), BF),
                sds((ent_rows, width), F32),
                sds((8, width), F32),
                sds((slots, width), BF),
            ],
        )
        if t + 1 < sections:
            collected[t + 1] = c
        ret = a2a(rep.reshape(groups, room, width), "ent").reshape(slots, width)
        ins = (ret, gp, osr, keep, w_gate, w_self, w_neigh)
        base, sp, *sends = run(
            functools.partial(back_kernel, sections),
            "back",
            ins,
            [whole(x) for x in ins],
            [sds((ent_rows, width), F32), sds((ent_rows, 2 * width), BF)]
            + [sds((ent_rows, width), BF)] * (sections - 1),
        )
        parts = [base] + [
            lax.ppermute(x, "hist", [(i, (i + k + 1) % sections) for i in range(sections)])
            for k, x in enumerate(sends)
        ]
        ins = (xg, gp, sp, ret, rid, bias) + (() if totals is None else tuple(totals))
        totals = run(
            functools.partial(grad_kernel, half, totals is None),
            "grad",
            ins,
            [block(xg.shape[1:], t)] + [whole(x) for x in ins[1:]],
            [
                sds((features, 2 * width), F32),
                sds((half, width), F32),
                sds((rel_rows, width), F32),
                sds((8, width), F32),
            ],
        )
    total = parts[0]
    for p in parts[1:]:
        total = total + p.astype(F32)
    collected[0] = total
    result = a2a(jnp.stack(collected), "hist")
    result = result.transpose(1, 0, 2).reshape(1, ent_rows, features)

    gs, ns, rs, bs = totals
    chunk = sum(sizes) + 16
    ins = (gs, ns, rs, qp, bs)
    (packed,) = run(
        functools.partial(pack_kernel, sizes),
        "pack",
        ins,
        [whole(x) for x in ins],
        [sds((groups, chunk, width), BF)],
    )
    landed = a2a(packed, "ent")
    pairs = groups // 2
    (copies,) = run(
        add_kernel, "sum", (landed,), [whole(landed)], [sds((pairs, chunk, width), BF)]
    )
    same = [[i for i in range(groups) if i % 2 == core] for core in range(2)]
    column = lax.all_to_all(
        copies, "ent", split_axis=0, concat_axis=0, tiled=True, axis_index_groups=same
    )
    rows = [column] + [
        lax.ppermute(column, "hist", [(i, (i + k) % sections) for i in range(sections)])
        for k in range(1, sections)
    ]
    other = lax.ppermute(
        jnp.concatenate(rows, axis=0), "ent", [(i, i ^ 1) for i in range(groups)]
    )
    ins = (*rows, other, w_neigh, relation)
    factor = 1.0 / math.sqrt(sections * ent_rows * groups)
    tall = [size * groups for size in sizes]
    grads = pl.pallas_call(
        functools.partial(last_kernel, sections, groups, sizes, factor),
        name="last",
        grid=(1,),
        in_specs=[whole(x) for x in ins],
        out_specs=[
            block(w_neigh.shape),
            block((tall[1], features)),
            block((tall[0], features)),
            block((8, features)),
            block((relations, features)),
        ],
        out_shape=[
            sds(w_neigh.shape, F32),
            sds((tall[1], features), F32),
            sds((tall[0], features), F32),
            sds((8, features), F32),
            sds((relations, features), F32),
        ],
        scratch_shapes=[
            pltpu.VMEM((tall[3], features), BF),
            pltpu.VMEM((tall[4], features), BF),
            pltpu.VMEM((tall[2], features), F32),
        ],
    )(*ins)
    neigh, self_, gate, bias, rel = grads
    return (
        result,
        neigh,
        self_[:features],
        gate[:features],
        bias[0],
        rel,
    )


def solution(mesh):
    return jax.shard_map(
        on_device,
        mesh=mesh,
        in_specs=(
            P("hist", "ent", None),
            P(),
            P(),
            P(),
            P(),
            P(),
            P("hist", "ent"),
            P("hist", "ent"),
            P("hist", "ent"),
            P("hist", "ent"),
            P("ent"),
            P("ent"),
            P("ent", None),
        ),
        out_specs=(P("hist", "ent", None), P(), P(), P(), P(), P()),
        check_vma=False,
    )
```

```python
import functools
import math

import jax
import jax.numpy as jnp
from jax import lax
from jax.experimental import pallas as pl
from jax.experimental.pallas import tpu as pltpu
from jax.sharding import PartitionSpec as P

BF = jnp.bfloat16
F32 = jnp.float32
TALL = (((0,), (0,)), ((), ()))
WIDE = (((1,), (1,)), ((), ()))
LANES = 128


def dot(a, b, dims=(((1,), (0,)), ((), ()))):
    return lax.dot_general(a, b, dims, preferred_element_type=F32)


def onehot(ids, rows):
    spot = lax.broadcasted_iota(jnp.int32, (rows, ids.shape[1]), 0)
    return jnp.where(spot == ids, 1.0, 0.0).astype(BF)


def round_up(value, step):
    return -(-value // step) * step


def block(shape, lead=None):
    if lead is None:
        return pl.BlockSpec(shape, lambda i: (0,) * len(shape))
    return pl.BlockSpec((None,) + shape, lambda i: (lead,) + (0,) * len(shape))


def whole(x):
    return block(x.shape)


def run(body, name, ins, specs, outs, scratch=()):
    return pl.pallas_call(
        body,
        name=name,
        grid=(1,),
        in_specs=specs,
        out_specs=[block(s.shape) for s in outs],
        out_shape=outs,
        scratch_shapes=list(scratch),
    )(*ins)


def sds(shape, dtype):
    return jax.ShapeDtypeStruct(shape, dtype)


def place(value, size):
    return pl.ds(pl.multiple_of(value * size, size), size)


def pre_kernel(x, src, rid, xp):
    ent_rows, features = x.shape
    ids = src[...]
    rids = rid[...]
    extra = jnp.zeros((8, features), F32)
    level = lax.broadcasted_iota(jnp.int32, (8, features), 0)
    for k in range(src.shape[1] // features):
        cut = slice(k * features, (k + 1) * features)
        for j, piece in enumerate((ids[:, cut], rids[:, cut] // 256, rids[:, cut] % 256)):
            extra = jnp.where(level == 3 * k + j, piece.astype(F32), extra)
    xp[:ent_rows, :] = x[...]
    xp[ent_rows:, :] = extra.astype(BF)


def send_kernel(sections, groups, x, rel, src, dst, rid, counts, msg):
    ent_rows, features = x.shape
    slots = src.shape[1]
    room = slots // groups
    width = features // sections
    e = lax.axis_index("ent")
    ids = src[...]
    rids = rid[...]
    xv = x[...]
    got = dot(onehot(ids, ent_rows), xv, TALL) + dot(onehot(rids, rel.shape[0]), rel[...], TALL)
    inputs = got.astype(BF)
    for target in range(sections):
        for u in range(groups):
            msg[target * groups + u, :room, :] = inputs[
                u * room : (u + 1) * room, target * width : (target + 1) * width
            ]
    lane = lax.broadcasted_iota(jnp.int32, (1, slots), 1)
    limit = jnp.zeros((1, slots), jnp.int32)
    for u in range(groups):
        limit = jnp.where(lane // room == u, counts[0, u], limit)
    live = jnp.where(lane % room < limit, dst[...], -1).astype(F32)
    per = width // room
    seat = lax.broadcasted_iota(jnp.int32, (8, width), 1) // room
    for u in range(groups):
        start = u * room // width * width
        row = jnp.broadcast_to(live[:, start : start + width], (8, width))
        turn = lax.rem(e - u + per * groups, per) * room
        row = pltpu.roll(row, turn, 1)
        row = jnp.where(seat == lax.rem(e, per), row, -1.0).astype(BF)
        for target in range(sections):
            msg[target * groups + u, room:, :] = row

def gather_kernel(count, *refs):
    for t in range(count):
        recv = refs[t]
        od, odt, scaling, summed_out = refs[count + 4 * t : count + 4 * t + 4]
        groups = recv.shape[0]
        width = recv.shape[2]
        room = recv.shape[1] - 8
        ent_rows = od.shape[0]
        per = width // room
        degree = jnp.zeros((ent_rows, width), F32)
        summed = jnp.zeros((ent_rows, width), F32)
        ones = jnp.ones((width, width), BF)
        for g in range(groups // per):
            ids = recv[g * per, room:, :].astype(F32)
            for j in range(1, per):
                ids = jnp.maximum(ids, recv[g * per + j, room:, :].astype(F32))
            hot = onehot(ids[:1].astype(jnp.int32), ent_rows)
            rows = jnp.concatenate([recv[g * per + j, :room, :] for j in range(per)], axis=0)
            summed = summed + dot(hot, rows)
            degree = degree + dot(hot, ones)
            od[:, g * width : (g + 1) * width] = hot
            odt[g * width : (g + 1) * width, :] = hot.astype(F32).T.astype(BF)
        scaling[...] = 1.0 / jnp.maximum(degree, 1.0)
        summed_out[...] = summed


def stacked(recv):
    return jnp.concatenate([recv[i, : recv.shape[1] - 8, :] for i in range(recv.shape[0])], axis=0)


def state_values(mates, xt, scaling, summed, od, mate_rows, wg, ws, wn, bias):
    ent_rows, width = summed.shape
    half = wn.shape[1]
    h = lax.axis_index("hist")
    cols = place(h, width)
    seat = lax.rem(h, mates)
    x = xt[:ent_rows, :]
    gathered = jnp.zeros((ent_rows, width), F32)
    for m in range(mates):
        part = summed[...] if m == 0 else dot(od[...], stacked(mate_rows[m - 1]))
        high = part.astype(BF)
        low = (part - high.astype(F32)).astype(BF)
        source = lax.rem(seat - m + mates, mates)
        w = wn[h * width // half, place(source, width), place(seat, width)]
        gathered = gathered + dot(
            jnp.concatenate([high, low], axis=1), jnp.concatenate([w, w], axis=0)
        )
    pre_act = gathered * scaling + dot(x, ws[:, cols])
    gate_open = jax.nn.sigmoid(dot(x, wg[:, cols]) + bias[:, cols])
    sig = jax.nn.sigmoid(pre_act)
    new_state = pre_act * sig
    shut = 1.0 - gate_open
    return (
        (new_state - xt[:ent_rows, cols].astype(F32)) * gate_open * shut,
        gate_open * (sig * (1.0 + pre_act * (1.0 - sig))),
        shut,
    )


def choose(t, sections, xs, xt):
    h = lax.axis_index("hist")
    for k in range(sections):

        @pl.when(lax.rem(h - k + sections, sections) == t)
        def _():
            xt[...] = xs[k][...]


def index_rows(xt, ent_rows, osr, rid):
    slots = osr.shape[1]
    features = xt.shape[1]
    extra = xt[ent_rows:, :].astype(F32).astype(jnp.int32)
    for k in range(slots // features):
        cut = slice(k * features, (k + 1) * features)
        osr[:, cut] = onehot(extra[3 * k : 3 * k + 1], ent_rows)
        ids = extra[3 * k + 1 : 3 * k + 2] * 256 + extra[3 * k + 2 : 3 * k + 3]
        rid[:, cut] = jnp.broadcast_to(ids, (8, features))


def state_kernel(t, sections, mates, *refs):
    xs = refs[:sections]
    mate_rows = refs[sections : sections + mates - 1]
    scaling, summed, od, wg, ws, wn, bias, al, be, ka, osr, rid, xt = refs[sections + mates - 1 :]
    choose(t, sections, xs, xt)
    values = state_values(mates, xt, scaling[...], summed, od, mate_rows, wg, ws, wn, bias)
    al[...], be[...], ka[...] = values
    index_rows(xt, summed.shape[0], osr, rid)


def query_kernel(qe, qr, qg, top, qp):
    width = top.shape[1]
    h = lax.axis_index("hist")
    grad = qg[:, place(h, width)]
    for ids, out in ((qe, top), (qr, qp)):
        hot = onehot(ids[...], out.shape[0]).astype(F32)
        out[...] = lax.dot_general(
            hot,
            grad,
            (((1,), (0,)), ((), ())),
            precision=lax.Precision.HIGHEST,
            preferred_element_type=F32,
        )


def arrived(parts, ret, osr):
    c = parts[0][...]
    for p in parts[1:]:
        c = c + p[...].astype(F32)
    slots = osr.shape[1]
    for m in range(ret.shape[0] // slots):
        c = c + dot(osr[...], ret[m * slots : (m + 1) * slots, :])
    return c


def step_kernel(sections, mates, first, *refs):
    if first:
        c = refs[0][...]
        refs = refs[1:]
    else:
        c = arrived(refs[:sections], refs[sections], refs[sections + 1])
        refs = refs[sections + 2 :]
    al, be, ka, scaling, odt, wg, ws, wn, c_out, gp, g_out, base, rep, bias, *sends = refs
    width = al.shape[1]
    half = wn.shape[1]
    slots = odt.shape[0]
    h = lax.axis_index("hist")
    gate_term = c * al[...]
    pre_term = c * be[...]
    g = (pre_term * scaling[...]).astype(BF)
    g_out[...] = g
    seat = lax.rem(h, mates)
    w = wn[h * width // half, :, place(seat, width)]
    out = dot(odt[...], dot(g, w, WIDE).astype(BF)).astype(BF)
    for m in range(mates):
        rep[m * slots : (m + 1) * slots, :] = out[:, m * width : (m + 1) * width]
    both = jnp.concatenate([gate_term.astype(BF), pre_term.astype(BF)], axis=1)
    gp[...] = both
    for k in range(sections):
        rows = place(lax.rem(h + k, sections), width)
        right = jnp.concatenate([wg[rows, place(h, width)], ws[rows, place(h, width)]], axis=1)
        out = dot(both, right, WIDE)
        if k == 0:
            base[...] = c * ka[...] + out
        else:
            sends[k - 1][...] = out.astype(BF)
    c_out[...] = c
    bias[...] = jnp.broadcast_to(jnp.sum(gate_term, axis=0, keepdims=True), bias.shape)


def grad_kernel(steps, mates, *refs):
    outs = refs[-3:]
    gs, ns, bs = outs
    deep = 5 + mates
    h = lax.axis_index("hist")
    for t in range(steps):
        xt, gp, bias, odt, g = refs[deep * t : deep * t + 5]
        rows = refs[deep * t + 5 : deep * (t + 1)]
        ent_rows, width = g.shape
        seat = lax.rem(h, mates)

        def put(out, at, value):
            out[at] = value if t == 0 else out[at] + value

        put(gs, ..., dot(xt[:ent_rows, :], gp[...], TALL))
        put(bs, ..., bias[...])
        replies = dot(odt[...], g[...]).astype(BF)
        for m in range(mates):
            source = lax.rem(seat - m + mates, mates)
            put(ns, place(source, width), dot(stacked(rows[m]), replies, TALL))


def rel_sum(count, refs, total):
    for t in range(count):
        ret, rid = refs[2 * t : 2 * t + 2]
        slots = rid.shape[1]
        hot = onehot(rid[:1, :], total.shape[0])
        for m in range(ret.shape[0] // slots):
            total = total + dot(hot, ret[m * slots : (m + 1) * slots, :])
    return total


def rel_kernel(count, *refs):
    old, out = refs[-2:]
    out[...] = rel_sum(count, refs, old[...])


def pack_kernel(sizes, relations, gs, ns, bs, ret, rid, old, mine, other, rs):
    pairs = mine.shape[0]
    width = mine.shape[2]
    core = lax.rem(lax.axis_index("ent"), 2)
    total = rel_sum(1, (ret, rid), old[...])
    level = lax.broadcasted_iota(jnp.int32, total.shape, 0)
    rs[...] = jnp.where(level == relations, bs[:1, :], total)
    pieces = (gs.at[:, :width], gs.at[:, width:], ns, rs)
    for u in range(2 * pairs):
        rows = []
        for piece, size in zip(pieces, sizes):
            deep = piece.shape[0]
            low = min(u * size, deep)
            high = min(low + size, deep)
            if high > low:
                rows.append(piece[low:high, :])
            if high - low < size:
                rows.append(jnp.zeros((size - high + low, width), F32))
        value = jnp.concatenate(rows, axis=0).astype(BF)

        @pl.when(core == u % 2)
        def _():
            mine[u // 2] = value

        @pl.when(core != u % 2)
        def _():
            other[u // 2] = value


def pair_kernel(a, b, out):
    out[...] = (a[...].astype(F32) + b[...].astype(F32)).astype(BF)


def add_kernel(x, out):
    total = x[0].astype(F32)
    for u in range(1, x.shape[0]):
        total = total + x[u].astype(F32)
    for k in range(out.shape[0]):
        out[k] = total.astype(BF)


def pick_kernel(sections, *refs):
    parts = refs[:sections]
    ret, osr = refs[sections : sections + 2]
    saved = refs[sections + 2 : 2 * sections + 1]
    outs = refs[2 * sections + 1 :]
    h = lax.axis_index("hist")
    c = arrived(parts, ret, osr)
    for k in range(sections):
        to = lax.rem(h + k, sections)

        @pl.when(to == 0)
        def _():
            outs[k][...] = c

        for t in range(1, sections):

            @pl.when(to == t)
            def _():
                outs[k][...] = saved[t - 1][...]


def last_kernel(sections, groups, mates, sizes, factor, *refs):
    mine = refs[:sections]
    other = refs[sections : 2 * sections]
    rows = refs[2 * sections : 3 * sections]
    result, neigh, self_, gate, bias, relation, n_all, r_all = refs[3 * sections :]
    width = mine[0].shape[2]
    relations = relation.shape[0]
    h = lax.axis_index("hist")
    core = lax.rem(lax.axis_index("ent"), 2)
    for k in range(sections):
        cols = place(lax.rem(h - k + sections, sections), width)
        result[:, cols] = rows[k][...]
        for z in range(groups // 2):
            for flip, piece in enumerate((mine[k], other[k])):
                u = 2 * z + (core if flip == 0 else 1 - core)
                at = 0
                for out, size in zip((gate, self_, n_all, r_all), sizes):
                    out[place(u, size), cols] = piece[z, at : at + size, :].astype(F32) * factor
                    at += size
    relation[...] = r_all[:relations, :]
    bias[...] = r_all[relations : relations + 1, :]
    half = neigh.shape[1]
    for f in range(sections):
        neigh[f // mates, :, f % mates * width : (f % mates + 1) * width] = n_all[
            :half, f * width : (f + 1) * width
        ]


def on_device(
    states,
    w_neigh,
    w_self,
    w_gate,
    b_gate,
    relation,
    edge_src,
    edge_rel,
    edge_dst,
    send_counts,
    query_ent,
    query_rel,
    query_grad,
):
    groups = lax.axis_size("ent")
    sections = lax.axis_size("hist")
    ent_rows, features = states.shape[1:]
    slots = edge_src.shape[1]
    room = slots // groups
    width = features // sections
    blocks, half = w_neigh.shape[:2]
    mates = sections // blocks
    relations = relation.shape[0]
    hidden = states[0]
    bias_row = b_gate.reshape(1, features)
    smem = pl.BlockSpec(memory_space=pltpu.SMEM)
    members = mates * groups
    block_groups = [list(range(b * members, (b + 1) * members)) for b in range(blocks)]

    def turn(x, k):
        return lax.ppermute(x, "hist", [(i, (i + k) % sections) for i in range(sections)])

    def to_mate(x, m):
        route = [(i, i // mates * mates + (i + m) % mates) for i in range(sections)]
        return lax.ppermute(x, "hist", route)

    def to_core(x):
        return lax.ppermute(x, "ent", [(i, i ^ 1) for i in range(groups)])

    rows_f32 = sds((ent_rows, width), F32)
    rows_bf = sds((ent_rows, width), BF)

    ins = (hidden, edge_src, edge_rel)
    (xp,) = run(
        pre_kernel, "pre", ins, [whole(x) for x in ins], [sds((ent_rows + 8, features), BF)]
    )
    xs = [xp] + [turn(xp, k) for k in range(1, sections)]
    (msg,) = run(
        functools.partial(send_kernel, sections, groups),
        "send",
        (hidden, relation, edge_src, edge_dst, edge_rel, send_counts),
        [whole(hidden), whole(relation)] + [whole(edge_src)] * 3 + [smem],
        [sds((sections * groups, room + 8, width), BF)],
    )
    recv = lax.all_to_all(
        msg, ("hist", "ent"), split_axis=0, concat_axis=0, tiled=True
    ).reshape(sections, groups, room + 8, width)
    last = sections - 1
    tops = recv[last]
    rest = recv[:last]
    mate_tops = [to_mate(tops, m) for m in range(1, mates)]
    mate_rest = [to_mate(rest, m) for m in range(1, mates)]

    rel_rows = round_up(relations + 1, 8)
    qe = query_ent.reshape(1, -1)
    qr = query_rel.reshape(1, -1)
    top, rs = run(
        query_kernel,
        "query",
        (qe, qr, query_grad),
        [whole(qe), whole(qr), whole(query_grad)],
        [rows_f32, sds((rel_rows, width), F32)],
    )

    def gather(arrays, specs, count):
        outs = run(
            functools.partial(gather_kernel, count),
            "gather",
            arrays,
            specs,
            [sds((ent_rows, slots), BF), sds((slots, ent_rows), BF), rows_f32, rows_f32] * count,
        )
        return [outs[4 * t : 4 * t + 4] for t in range(count)]

    gathered = gather(
        (rest,) * last, [block(rest.shape[1:], t) for t in range(last)], last
    ) + gather((tops,), [whole(tops)], 1)

    def pick_t(arrays, tops, t):
        if t == last:
            return list(tops), [whole(x) for x in tops]
        return list(arrays), [block(x.shape[1:], t) for x in arrays]

    def prepare(t):
        od, odt, scaling, summed = gathered[t]
        mate, mate_specs = pick_t(mate_rest, mate_tops, t)
        ins = (scaling, summed, od, w_gate, w_self, w_neigh, bias_row)
        al, be, ka, osr, rid, xt = run(
            functools.partial(state_kernel, t, sections, mates),
            "state",
            (*xs, *mate, *ins),
            [whole(x) for x in xs] + mate_specs + [whole(x) for x in ins],
            [rows_f32] * 3
            + [
                sds((ent_rows, slots), BF),
                sds((8, slots), jnp.int32),
                sds((ent_rows + 8, features), BF),
            ],
        )
        return al, be, ka, scaling, odt, osr, rid, xt

    saved = [None] * (sections + 1)
    grad_ins, grad_specs, rel_ins = [], [], []
    for t in range(last, -1, -1):
        al, be, ka, scaling, odt, osr, rid, xt = prepare(t)
        came = (top,) if t == last else (*parts, ret, osr_before)
        ins = (*came, al, be, ka, scaling, odt, w_gate, w_self, w_neigh)
        c, gp, g, base, rep, bias, *sends = run(
            functools.partial(step_kernel, sections, mates, t == last),
            "step",
            ins,
            [whole(x) for x in ins],
            [rows_f32, sds((ent_rows, 2 * width), BF), rows_bf, rows_f32]
            + [sds((mates * slots, width), BF), sds((8, width), F32)]
            + [rows_bf] * (sections - 1),
        )
        saved[t + 1] = c
        ret = lax.all_to_all(
            rep.reshape(members, room, width),
            ("hist", "ent"),
            split_axis=0,
            concat_axis=0,
            tiled=True,
            axis_index_groups=block_groups,
        ).reshape(mates * slots, width)
        parts = [base] + [turn(x, k + 1) for k, x in enumerate(sends)]
        osr_before = osr
        rows, rows_specs = pick_t((rest, *mate_rest), (tops, *mate_tops), t)
        ins = (xt, gp, bias, odt, g)
        grad_ins += [*ins, *rows]
        grad_specs += [whole(x) for x in ins] + rows_specs
        rel_ins += [ret, rid]

    gs, ns, bs = run(
        functools.partial(grad_kernel, sections, mates),
        "grad",
        grad_ins,
        grad_specs,
        [sds((features, 2 * width), F32), sds((half, width), F32), sds((8, width), F32)],
    )
    ins = (*rel_ins[:-2], rs)
    (rs,) = run(
        functools.partial(rel_kernel, last),
        "rel",
        ins,
        [whole(x) for x in ins],
        [sds((rel_rows, width), F32)],
    )

    ins = (*parts, ret, osr_before, *saved[1:sections])
    picks = run(
        functools.partial(pick_kernel, sections),
        "pick",
        ins,
        [whole(x) for x in ins],
        [rows_f32] * sections,
    )
    home = [picks[0]] + [turn(picks[k], k) for k in range(1, sections)]

    sizes = tuple(
        round_up(-(-rows // groups), 16) for rows in (features, features, half, rel_rows)
    )
    chunk = sum(sizes)
    pairs = groups // 2
    ins = (gs, ns, bs, ret, rid, rs)
    mine, other = run(
        functools.partial(pack_kernel, sizes, relations),
        "pack",
        ins,
        [whole(x) for x in ins],
        [sds((pairs, chunk, width), BF)] * 2,
        [pltpu.VMEM((rel_rows, width), F32)],
    )
    ins = (mine, to_core(other))
    (landed,) = run(
        pair_kernel, "pair", ins, [whole(x) for x in ins], [sds((pairs, chunk, width), BF)]
    )
    same = [[i for i in range(groups) if i % 2 == core] for core in range(2)]

    def a2a_same(x):
        return lax.all_to_all(
            x, "ent", split_axis=0, concat_axis=0, tiled=True, axis_index_groups=same
        )

    landed, home = lax.optimization_barrier((a2a_same(landed), home))
    (copies,) = run(
        add_kernel, "sum", (landed,), [whole(landed)], [sds((pairs, chunk, width), BF)]
    )
    column = a2a_same(copies)
    mine = [column] + [turn(column, k) for k in range(1, sections)]
    other = [to_core(x) for x in mine]
    ins = (*mine, *other, *home)
    factor = 1.0 / math.sqrt(sections * ent_rows * groups)
    tall = [size * groups for size in sizes]
    result, neigh, self_, gate, bias, rel = pl.pallas_call(
        functools.partial(last_kernel, sections, groups, mates, sizes, factor),
        name="last",
        grid=(1,),
        in_specs=[whole(x) for x in ins],
        out_specs=[
            block((ent_rows, features)),
            block(w_neigh.shape),
            block((tall[1], features)),
            block((tall[0], features)),
            block((1, features)),
            block((relations, features)),
        ],
        out_shape=[
            sds((ent_rows, features), F32),
            sds(w_neigh.shape, F32),
            sds((tall[1], features), F32),
            sds((tall[0], features), F32),
            sds((1, features), F32),
            sds((relations, features), F32),
        ],
        scratch_shapes=[
            pltpu.VMEM((tall[2], features), F32),
            pltpu.VMEM((tall[3], features), F32),
        ],
    )(*ins)
    return (
        result[None],
        neigh,
        self_[:features],
        gate[:features],
        bias.reshape(features),
        rel,
    )


def solution(mesh):
    return jax.shard_map(
        on_device,
        mesh=mesh,
        in_specs=(
            P("hist", "ent", None),
            P(),
            P(),
            P(),
            P(),
            P(),
            P("hist", "ent"),
            P("hist", "ent"),
            P("hist", "ent"),
            P("hist", "ent"),
            P("ent"),
            P("ent"),
            P("ent", None),
        ),
        out_specs=(P("hist", "ent", None), P(), P(), P(), P(), P()),
        check_vma=False,
    )
```

```python
import functools
import math

import jax
import jax.numpy as jnp
from jax import lax
from jax.experimental import pallas as pl
from jax.experimental.pallas import tpu as pltpu
from jax.sharding import PartitionSpec as P

BF = jnp.bfloat16
F32 = jnp.float32
TALL = (((0,), (0,)), ((), ()))
WIDE = (((1,), (1,)), ((), ()))
LANES = 128


def dot(a, b, dims=(((1,), (0,)), ((), ()))):
    return lax.dot_general(a, b, dims, preferred_element_type=F32)


def onehot(ids, rows):
    spot = lax.broadcasted_iota(jnp.int32, (rows, ids.shape[1]), 0)
    return jnp.where(spot == ids, 1.0, 0.0).astype(BF)


class Far:
    def __init__(self, value):
        self.value = value
        self.shape = value.shape


def raw(x):
    return x.value if isinstance(x, Far) else x


def far(x):
    return x if isinstance(x, Far) else Far(x)


def round_up(value, step):
    return -(-value // step) * step


def block(shape, lead=None):
    if lead is None:
        return pl.BlockSpec(shape, lambda i: (0,) * len(shape))
    return pl.BlockSpec((None,) + shape, lambda i: (lead,) + (0,) * len(shape))


def whole(x):
    return block(x.shape)


def run(body, name, ins, specs, outs, scratch=(), limit=16):
    tiled = any(s.block_shape and None in s.block_shape for s in specs)
    near = pl.BlockSpec(memory_space=pltpu.VMEM)

    def spec(s):
        return near if s.block_shape and not tiled else s

    arrays = [
        pltpu.with_memory_space_constraint(x.value, pltpu.HBM) if isinstance(x, Far) else x
        for x in ins
    ]
    shapes = [
        pltpu.HBM(o.value.shape, o.value.dtype) if isinstance(o, Far) else o for o in outs
    ]
    results = pl.pallas_call(
        body,
        name=name,
        in_specs=[spec(s) for s in specs],
        out_specs=[spec(block(o.shape)) for o in shapes],
        out_shape=shapes,
        scratch_shapes=list(scratch),
        compiler_params=pltpu.CompilerParams(vmem_limit_bytes=limit << 20),
        **({"grid": (1,)} if tiled else {}),
    )(*arrays)
    return [Far(r) if isinstance(o, Far) else r for r, o in zip(results, outs)]


def sds(shape, dtype):
    return jax.ShapeDtypeStruct(shape, dtype)


def place(value, size):
    return pl.ds(pl.multiple_of(value * size, size), size)


def pre_kernel(x, src, rid, xp):
    ent_rows, features = x.shape
    ids = src[...]
    rids = rid[...]
    extra = jnp.zeros((8, features), F32)
    level = lax.broadcasted_iota(jnp.int32, (8, features), 0)
    for k in range(src.shape[1] // features):
        cut = slice(k * features, (k + 1) * features)
        for j, piece in enumerate((ids[:, cut], rids[:, cut] // 256, rids[:, cut] % 256)):
            extra = jnp.where(level == 3 * k + j, piece.astype(F32), extra)
    xp[:ent_rows, :] = x[...]
    xp[ent_rows:, :] = extra.astype(BF)


def send_kernel(sections, groups, x, rel, src, dst, rid, counts, msg):
    ent_rows, features = x.shape
    slots = src.shape[1]
    room = slots // groups
    width = features // sections
    e = lax.axis_index("ent")
    ids = src[...]
    rids = rid[...]
    xv = x[...]
    got = dot(onehot(ids, ent_rows), xv, TALL) + dot(onehot(rids, rel.shape[0]), rel[...], TALL)
    inputs = got.astype(BF)
    for target in range(sections):
        for u in range(groups):
            msg[target * groups + u, :room, :] = inputs[
                u * room : (u + 1) * room, target * width : (target + 1) * width
            ]
    lane = lax.broadcasted_iota(jnp.int32, (1, slots), 1)
    limit = jnp.zeros((1, slots), jnp.int32)
    for u in range(groups):
        limit = jnp.where(lane // room == u, counts[0, u], limit)
    live = jnp.where(lane % room < limit, dst[...], -1).astype(F32)
    per = width // room
    seat = lax.broadcasted_iota(jnp.int32, (8, width), 1) // room
    for u in range(groups):
        start = u * room // width * width
        row = jnp.broadcast_to(live[:, start : start + width], (8, width))
        turn = lax.rem(e - u + per * groups, per) * room
        row = pltpu.roll(row, turn, 1)
        row = jnp.where(seat == lax.rem(e, per), row, -1.0).astype(BF)
        for target in range(sections):
            msg[target * groups + u, room:, :] = row

def stacked(recv):
    return jnp.concatenate([recv[i, : recv.shape[1] - 8, :] for i in range(recv.shape[0])], axis=0)


def choose(t, sections, act):
    h = lax.axis_index("hist")
    for k in range(sections):

        @pl.when(lax.rem(h - k + sections, sections) == t)
        def _():
            act(k)


def state_kernel(t, sections, mates, *refs):
    xs = refs[:sections]
    recv = refs[sections]
    mate_rows = refs[sections + 1 : sections + mates]
    wcat, wnc, bias, coef, odt, osr, rid, xt, sem = refs[sections + mates :]
    choose(t, sections, lambda k: pltpu.make_async_copy(xs[k], xt, sem).start())
    groups, deep, width = recv.shape
    room = deep - 8
    slots, ent_rows = odt.shape
    per = width // room
    h = lax.axis_index("hist")
    seat = lax.rem(h, mates)
    degree = jnp.zeros((ent_rows, width), F32)
    summed = [jnp.zeros((ent_rows, width), F32) for m in range(mates)]
    ones = jnp.ones((width, width), BF)
    for g in range(groups // per):
        ids = recv[g * per, room:, :].astype(F32)
        for j in range(1, per):
            ids = jnp.maximum(ids, recv[g * per + j, room:, :].astype(F32))
        hot = onehot(ids[:1].astype(jnp.int32), ent_rows)
        degree = degree + dot(hot, ones)
        for m, source in enumerate((recv, *mate_rows)):
            rows = jnp.concatenate([source[g * per + j, :room, :] for j in range(per)], axis=0)
            summed[m] = summed[m] + dot(hot, rows)
        odt[g * width : (g + 1) * width, :] = hot.astype(F32).T.astype(BF)
    gathered = jnp.zeros((ent_rows, width), F32)
    for m in range(mates):
        high = summed[m].astype(BF)
        low = (summed[m] - high.astype(F32)).astype(BF)
        w = wnc[place(lax.rem(seat - m + mates, mates), width), :]
        gathered = gathered + dot(
            jnp.concatenate([high, low], axis=1), jnp.concatenate([w, w], axis=0)
        )
    scaling = 1.0 / jnp.maximum(degree, 1.0)
    coef[:, 3 * width :] = scaling
    pltpu.make_async_copy(xs[0], xt, sem).wait()
    straight = dot(xt[:ent_rows, :], wcat[...])
    gate_open = jax.nn.sigmoid(straight[:, :width] + bias[:1, :])
    pre_act = gathered * scaling + straight[:, width:]
    sig = jax.nn.sigmoid(pre_act)
    new_state = pre_act * sig
    shut = 1.0 - gate_open
    hidden = xt[:ent_rows, place(h, width)].astype(F32)
    coef[:, :width] = (new_state - hidden) * gate_open * shut
    coef[:, width : 2 * width] = gate_open * (sig * (1.0 + pre_act * (1.0 - sig)))
    coef[:, 2 * width : 3 * width] = shut
    features = xt.shape[1]
    extra = xt[ent_rows:, :].astype(F32).astype(jnp.int32)
    for k in range(slots // features):
        cut = slice(k * features, (k + 1) * features)
        osr[:, cut] = onehot(extra[3 * k : 3 * k + 1], ent_rows)
        ids = extra[3 * k + 1 : 3 * k + 2] * 256 + extra[3 * k + 2 : 3 * k + 3]
        rid[:, cut] = jnp.broadcast_to(ids, (8, features))


def query_kernel(qe, qr, qg, wg, ws, wn, bias, top, qp, wcat, wnc, bias_out):
    width = top.shape[1]
    half, mates = wn.shape[1], wn.shape[1] // width
    h = lax.axis_index("hist")
    cols = place(h, width)
    wcat[:, :width] = wg[:, cols]
    wcat[:, width:] = ws[:, cols]
    wnc[...] = wn[h * width // half, :, place(lax.rem(h, mates), width)]
    bias_out[...] = jnp.broadcast_to(bias[:, cols], bias_out.shape)
    grad = qg[:, cols]
    for ids, out in ((qe, top), (qr, qp)):
        hot = onehot(ids[...], out.shape[0]).astype(F32)
        out[...] = lax.dot_general(
            hot,
            grad,
            (((1,), (0,)), ((), ())),
            precision=lax.Precision.HIGHEST,
            preferred_element_type=F32,
        )


def arrived(parts, ret, osr):
    width = ret.shape[1]
    c = parts[0][:, width:]
    for p in parts[1:]:
        c = c + p[...].astype(F32)
    slots = osr.shape[1]
    for m in range(ret.shape[0] // slots):
        c = c + dot(osr[...], ret[m * slots : (m + 1) * slots, :])
    return c


def step_kernel(sections, mates, first, *refs):
    if first:
        c = refs[0][...]
        refs = refs[1:]
    else:
        c = arrived(refs[:sections], refs[sections], refs[sections + 1])
        refs = refs[sections + 2 :]
    coef, odt, wcat, wnc, pair, low, rep, bias, *sends = refs
    slots = odt.shape[0]
    width = rep.shape[1]
    h = lax.axis_index("hist")
    gate_term = c * coef[:, :width]
    pre_term = c * coef[:, width : 2 * width]
    g = (pre_term * coef[:, 3 * width :]).astype(BF)
    low[:, 2 * width :] = g
    out = dot(odt[...], dot(g, wnc[...], WIDE).astype(BF)).astype(BF)
    for m in range(mates):
        rep[m * slots : (m + 1) * slots, :] = out[:, m * width : (m + 1) * width]
    both = jnp.concatenate([gate_term.astype(BF), pre_term.astype(BF)], axis=1)
    low[:, : 2 * width] = both
    for k in range(sections):
        out = dot(both, wcat[place(lax.rem(h + k, sections), width), :], WIDE)
        if k == 0:
            pair[:, width:] = c * coef[:, 2 * width : 3 * width] + out
        else:
            sends[k - 1][...] = out.astype(BF)
    pair[:, :width] = c
    bias[...] = jnp.broadcast_to(jnp.sum(gate_term, axis=0, keepdims=True), bias.shape)


def grad_kernel(steps, mates, *refs):
    xs = refs[:steps]
    refs = refs[steps:]
    gs, ns, bs, held = refs[-4:]
    deep = 3 + mates
    h = lax.axis_index("hist")
    for t in range(steps):
        snapshot = steps - 1 - t
        low, bias, odt = refs[deep * t : deep * t + 3]
        rows = refs[deep * t + 3 : deep * (t + 1)]
        ent_rows = low.shape[0]
        width = low.shape[1] // 3
        seat = lax.rem(h, mates)

        def put(out, at, value):
            out[at] = value if t == 0 else out[at] + value

        held[snapshot] = low[:, : 2 * width]
        put(bs, ..., bias[...])
        replies = dot(odt[...], low[:, 2 * width :]).astype(BF)
        for m in range(mates):
            source = lax.rem(seat - m + mates, mates)
            put(ns, place(source, width), dot(stacked(rows[m]), replies, TALL))
    for k in range(steps):
        value = dot(xs[k][:ent_rows, :], held[lax.rem(h - k + steps, steps)], TALL)
        gs[...] = value if k == 0 else gs[...] + value


def rel_sum(count, refs, total):
    for t in range(count):
        ret, rid = refs[2 * t : 2 * t + 2]
        slots = rid.shape[1]
        hot = onehot(rid[:1, :], total.shape[0])
        for m in range(ret.shape[0] // slots):
            total = total + dot(hot, ret[m * slots : (m + 1) * slots, :])
    return total


def rel_kernel(count, *refs):
    old, out = refs[-2:]
    out[...] = rel_sum(count, refs, old[...])


def pack_kernel(sizes, relations, gs, ns, bs, ret, rid, old, mine, other, rs):
    pairs = mine.shape[0]
    width = mine.shape[2]
    core = lax.rem(lax.axis_index("ent"), 2)
    total = rel_sum(1, (ret, rid), old[...])
    level = lax.broadcasted_iota(jnp.int32, total.shape, 0)
    rs[...] = jnp.where(level == relations, bs[:1, :], total)
    pieces = (gs.at[:, :width], gs.at[:, width:], ns, rs)
    for u in range(2 * pairs):
        rows = []
        for piece, size in zip(pieces, sizes):
            deep = piece.shape[0]
            low = min(u * size, deep)
            high = min(low + size, deep)
            if high > low:
                rows.append(piece[low:high, :])
            if high - low < size:
                rows.append(jnp.zeros((size - high + low, width), F32))
        value = jnp.concatenate(rows, axis=0).astype(BF)

        @pl.when(core == u % 2)
        def _():
            mine[u // 2] = value

        @pl.when(core != u % 2)
        def _():
            other[u // 2] = value


def pair_kernel(a, b, out):
    out[...] = (a[...].astype(F32) + b[...].astype(F32)).astype(BF)


def add_kernel(x, out):
    total = x[0].astype(F32)
    for u in range(1, x.shape[0]):
        total = total + x[u].astype(F32)
    for k in range(out.shape[0]):
        out[k] = total.astype(BF)


def pick_kernel(sections, *refs):
    parts = refs[:sections]
    ret, osr = refs[sections : sections + 2]
    saved = refs[sections + 2 : 2 * sections + 1]
    outs = refs[2 * sections + 1 :]
    h = lax.axis_index("hist")
    c = arrived(parts, ret, osr)
    for k in range(sections):
        to = lax.rem(h + k, sections)

        @pl.when(to == 0)
        def _():
            outs[k][...] = c

        for t in range(1, sections):

            @pl.when(to == t)
            def _():
                outs[k][...] = saved[t - 1][:, : c.shape[1]]


def last_kernel(sections, groups, mates, sizes, factor, *refs):
    mine = refs[:sections]
    other = refs[sections : 2 * sections]
    rows = refs[2 * sections : 3 * sections]
    result, neigh, self_, gate, bias, relation, n_all, r_all = refs[3 * sections :]
    width = mine[0].shape[2]
    relations = relation.shape[0]
    h = lax.axis_index("hist")
    core = lax.rem(lax.axis_index("ent"), 2)
    for k in range(sections):
        cols = place(lax.rem(h - k + sections, sections), width)
        result[:, cols] = rows[k][...]
        for z in range(groups // 2):
            for flip, piece in enumerate((mine[k], other[k])):
                u = 2 * z + (core if flip == 0 else 1 - core)
                at = 0
                for out, size in zip((gate, self_, n_all, r_all), sizes):
                    out[place(u, size), cols] = piece[z, at : at + size, :].astype(F32) * factor
                    at += size
    relation[...] = r_all[:relations, :]
    bias[...] = r_all[relations : relations + 1, :]
    half = neigh.shape[1]
    for f in range(sections):
        neigh[f // mates, :, f % mates * width : (f % mates + 1) * width] = n_all[
            :half, f * width : (f + 1) * width
        ]


def on_device(
    states,
    w_neigh,
    w_self,
    w_gate,
    b_gate,
    relation,
    edge_src,
    edge_rel,
    edge_dst,
    send_counts,
    query_ent,
    query_rel,
    query_grad,
):
    groups = lax.axis_size("ent")
    sections = lax.axis_size("hist")
    ent_rows, features = states.shape[1:]
    slots = edge_src.shape[1]
    room = slots // groups
    width = features // sections
    blocks, half = w_neigh.shape[:2]
    mates = sections // blocks
    relations = relation.shape[0]
    hidden = far(states[0])
    relation, edge_src, edge_rel, edge_dst = map(far, (relation, edge_src, edge_rel, edge_dst))
    bias_row = b_gate.reshape(1, features)
    smem = pl.BlockSpec(memory_space=pltpu.SMEM)
    members = mates * groups
    block_groups = [list(range(b * members, (b + 1) * members)) for b in range(blocks)]

    def turn(x, k):
        return lax.ppermute(x, "hist", [(i, (i + k) % sections) for i in range(sections)])

    def to_mate(x, m):
        route = [(i, i // mates * mates + (i + m) % mates) for i in range(sections)]
        return lax.ppermute(x, "hist", route)

    def to_core(x):
        return lax.ppermute(x, "ent", [(i, i ^ 1) for i in range(groups)])

    rows_f32 = sds((ent_rows, width), F32)
    rows_bf = sds((ent_rows, width), BF)
    last = sections - 1

    ins = (hidden, edge_src, edge_rel)
    (xp,) = run(
        pre_kernel, "pre", ins, [whole(x) for x in ins], [far(sds((ent_rows + 8, features), BF))]
    )
    xs = [xp] + [far(turn(raw(xp), k)) for k in range(1, sections)]
    (msg,) = run(
        functools.partial(send_kernel, sections, groups),
        "send",
        (hidden, relation, edge_src, edge_dst, edge_rel, send_counts),
        [whole(hidden), whole(relation)] + [whole(edge_src)] * 3 + [smem],
        [far(sds((sections * groups, room + 8, width), BF))],
    )
    recv = lax.all_to_all(
        raw(msg), ("hist", "ent"), split_axis=0, concat_axis=0, tiled=True
    ).reshape(sections, groups, room + 8, width)

    rel_rows = round_up(relations + 1, 8)
    qe = query_ent.reshape(1, -1)
    qr = query_rel.reshape(1, -1)
    ins = tuple(map(far, (qe, qr, query_grad, w_gate, w_self, w_neigh, bias_row)))
    top, rs, wcat, wnc, bias_cols = run(
        query_kernel,
        "query",
        ins,
        [whole(x) for x in ins],
        [
            far(x)
            for x in (
                rows_f32,
                sds((rel_rows, width), F32),
                sds((features, 2 * width), BF),
                sds((half, width), BF),
                sds((8, width), F32),
            )
        ],
    )
    recv, held = lax.optimization_barrier((recv, raw(wnc)))
    wnc = far(held)
    came_rows = [recv[t] for t in range(sections)]
    mate_rows = [[to_mate(x, m) for m in range(1, mates)] for x in came_rows]
    any_space = pl.BlockSpec(memory_space=pl.ANY)

    def prepare(t, *after):
        received = came_rows[t] if t == last else far(came_rows[t])
        ins = (*xs, received, *mate_rows[t], wcat, wnc, bias_cols)
        return run(
            functools.partial(state_kernel, t, sections, mates),
            "state",
            ins,
            [any_space for x in xs] + [whole(x) for x in ins[sections:]],
            [
                far(x)
                for x in (
                    sds((ent_rows, 4 * width), F32),
                    sds((slots, ent_rows), BF),
                    sds((ent_rows, slots), BF),
                    sds((8, slots), jnp.int32),
                )
            ],
            [pltpu.VMEM((ent_rows + 8, features), BF), pltpu.SemaphoreType.DMA],
        )

    saved = [None] * (sections + 1)
    grad_ins, rel_ins = list(xs), []
    for t in range(last, -1, -1):
        coef, odt, osr, rid = prepare(t)
        if t > 0:
            held, *mate_rows[t - 1] = lax.optimization_barrier((raw(coef), *mate_rows[t - 1]))
            coef = far(held)
        came = (top,) if t == last else (*parts, ret, osr_before)
        ins = (*came, coef, odt, wcat, wnc)
        pair, low, rep, bias, *sends = run(
            functools.partial(step_kernel, sections, mates, t == last),
            "step",
            ins,
            [whole(x) for x in ins],
            [
                far(x)
                for x in (
                    sds((ent_rows, 2 * width), F32),
                    sds((ent_rows, 3 * width), BF),
                    sds((mates * slots, width), BF),
                    sds((8, width), F32),
                    *[rows_bf] * (sections - 1),
                )
            ],
        )
        saved[t + 1] = pair
        ret = lax.all_to_all(
            raw(rep).reshape(members, room, width),
            ("hist", "ent"),
            split_axis=0,
            concat_axis=0,
            tiled=True,
            axis_index_groups=block_groups,
        ).reshape(mates * slots, width)
        parts = [pair] + [turn(raw(x), k + 1) for k, x in enumerate(sends)]
        osr_before = osr
        ins = (low, bias, odt, came_rows[t], *mate_rows[t])
        grad_ins += [far(x) for x in ins]
        rel_ins += [far(ret), rid]

    gs, ns, bs = run(
        functools.partial(grad_kernel, sections, mates),
        "grad",
        grad_ins,
        [whole(x) for x in grad_ins],
        [far(sds((features, 2 * width), F32)), far(sds((half, width), F32)), far(sds((8, width), F32))],
        [pltpu.VMEM((sections, ent_rows, 2 * width), BF)],
    )
    ins = (*rel_ins[:-2], rs)
    (rs,) = run(
        functools.partial(rel_kernel, last),
        "rel",
        ins,
        [whole(x) for x in ins],
        [far(sds((rel_rows, width), F32))],
    )
    sizes = tuple(
        round_up(-(-rows // groups), 16) for rows in (features, features, half, rel_rows)
    )
    chunk = sum(sizes)
    pairs = groups // 2
    ins = (gs, ns, bs, ret, rid, rs)
    ins = tuple(ins)
    mine, other = run(
        functools.partial(pack_kernel, sizes, relations),
        "pack",
        ins,
        [whole(x) for x in ins],
        [sds((pairs, chunk, width), BF)] * 2,
        [pltpu.VMEM((rel_rows, width), F32)],
    )
    ins = (mine, to_core(other))
    (landed,) = run(
        pair_kernel, "pair", ins, [whole(x) for x in ins], [sds((pairs, chunk, width), BF)]
    )
    same = [[i for i in range(groups) if i % 2 == core] for core in range(2)]

    def a2a_same(x):
        return lax.all_to_all(
            x, "ent", split_axis=0, concat_axis=0, tiled=True, axis_index_groups=same
        )

    landed, *moved = lax.optimization_barrier((a2a_same(landed), *parts[1:]))
    parts = [parts[0], *moved]
    (copies,) = run(
        add_kernel, "sum", (landed,), [whole(landed)], [sds((pairs, chunk, width), BF)]
    )
    ins = (*parts, ret, osr_before, *saved[1:sections])
    picks = run(
        functools.partial(pick_kernel, sections),
        "pick",
        ins,
        [whole(x) for x in ins],
        [rows_f32] * sections,
    )
    home = [picks[0]] + [turn(picks[k], k) for k in range(1, sections)]
    column, *home = lax.optimization_barrier((a2a_same(copies), *home))
    mine = [column] + [turn(column, k) for k in range(1, sections)]
    other = [to_core(x) for x in mine]
    ins = (*mine, *other, *home)
    factor = 1.0 / math.sqrt(sections * ent_rows * groups)
    tall = [size * groups for size in sizes]
    result, neigh, self_, gate, bias, rel = pl.pallas_call(
        functools.partial(last_kernel, sections, groups, mates, sizes, factor),
        name="last",
        compiler_params=pltpu.CompilerParams(vmem_limit_bytes=24 << 20),
        grid=(1,),
        in_specs=[whole(x) for x in ins],
        out_specs=[
            block((ent_rows, features)),
            block(w_neigh.shape),
            block((tall[1], features)),
            block((tall[0], features)),
            block((1, features)),
            block((relations, features)),
        ],
        out_shape=[
            sds((ent_rows, features), F32),
            sds(w_neigh.shape, F32),
            sds((tall[1], features), F32),
            sds((tall[0], features), F32),
            sds((1, features), F32),
            sds((relations, features), F32),
        ],
        scratch_shapes=[
            pltpu.VMEM((tall[2], features), F32),
            pltpu.VMEM((tall[3], features), F32),
        ],
    )(*ins)
    return (
        result[None],
        neigh,
        self_[:features],
        gate[:features],
        bias.reshape(features),
        rel,
    )


def solution(mesh):
    return jax.shard_map(
        on_device,
        mesh=mesh,
        in_specs=(
            P("hist", "ent", None),
            P(),
            P(),
            P(),
            P(),
            P(),
            P("hist", "ent"),
            P("hist", "ent"),
            P("hist", "ent"),
            P("hist", "ent"),
            P("ent"),
            P("ent"),
            P("ent", None),
        ),
        out_specs=(P("hist", "ent", None), P(), P(), P(), P(), P()),
        check_vma=False,
    )
```

```python
import functools
import math

import jax
import jax.numpy as jnp
from jax import lax
from jax.experimental import pallas as pl
from jax.experimental.pallas import tpu as pltpu
from jax.sharding import PartitionSpec as P


BF = jnp.bfloat16
F32 = jnp.float32
TALL = (((0,), (0,)), ((), ()))
WIDE = (((1,), (1,)), ((), ()))


def dot(a, b, dims=(((1,), (0,)), ((), ()))):
    return lax.dot_general(a, b, dims, preferred_element_type=F32)


def onehot(ids, rows):
    spot = lax.broadcasted_iota(jnp.int32, (rows, ids.shape[1]), 0)
    return jnp.where(spot == ids, 1.0, 0.0).astype(BF)


class Far:
    def __init__(self, value):
        self.value = value
        self.shape = value.shape


def raw(x):
    return x.value if isinstance(x, Far) else x


def far(x):
    return x if isinstance(x, Far) else Far(x)


def round_up(value, step):
    return -(-value // step) * step


def block(shape, lead=None):
    if lead is None:
        return pl.BlockSpec(shape, lambda i: (0,) * len(shape))
    return pl.BlockSpec((None,) + shape, lambda i: (lead,) + (0,) * len(shape))


def whole(x):
    return block(x.shape)


def run(body, ins, specs, outs, scratch=(), limit=16):
    tiled = any(s.block_shape and None in s.block_shape for s in specs)
    near = pl.BlockSpec(memory_space=pltpu.VMEM)

    def spec(s):
        return near if s.block_shape and not tiled else s

    arrays = [
        pltpu.with_memory_space_constraint(x.value, pltpu.HBM) if isinstance(x, Far) else x
        for x in ins
    ]
    shapes = [
        pltpu.HBM(o.value.shape, o.value.dtype) if isinstance(o, Far) else o for o in outs
    ]
    results = pl.pallas_call(
        body,
        in_specs=[spec(s) for s in specs],
        out_specs=[spec(block(o.shape)) for o in shapes],
        out_shape=shapes,
        scratch_shapes=list(scratch),
        compiler_params=pltpu.CompilerParams(vmem_limit_bytes=limit << 20),
        **({"grid": (1,)} if tiled else {}),
    )(*arrays)
    return [Far(r) if isinstance(o, Far) else r for r, o in zip(results, outs)]


def sds(shape, dtype):
    return jax.ShapeDtypeStruct(shape, dtype)


def place(value, size):
    return pl.ds(pl.multiple_of(value * size, size), size)


def pre_kernel(x, src, rid, xp):
    ent_rows, features = x.shape
    ids = src[...]
    rids = rid[...]
    extra = jnp.zeros((8, features), F32)
    level = lax.broadcasted_iota(jnp.int32, (8, features), 0)
    for k in range(src.shape[1] // features):
        cut = slice(k * features, (k + 1) * features)
        for j, piece in enumerate((ids[:, cut], rids[:, cut] // 256, rids[:, cut] % 256)):
            extra = jnp.where(level == 3 * k + j, piece.astype(F32), extra)
    xp[:ent_rows, :] = x[...]
    xp[ent_rows:, :] = extra.astype(BF)


def send_kernel(sections, groups, x, rel, src, dst, rid, counts, msg):
    ent_rows, features = x.shape
    slots = src.shape[1]
    room = slots // groups
    width = features // sections
    e = lax.axis_index("ent")
    ids = src[...]
    rids = rid[...]
    xv = x[...]
    got = dot(onehot(ids, ent_rows), xv, TALL) + dot(onehot(rids, rel.shape[0]), rel[...], TALL)
    inputs = got.astype(BF)
    for target in range(sections):
        for u in range(groups):
            msg[target * groups + u, :room, :] = inputs[
                u * room : (u + 1) * room, target * width : (target + 1) * width
            ]
    lane = lax.broadcasted_iota(jnp.int32, (1, slots), 1)
    limit = jnp.zeros((1, slots), jnp.int32)
    for u in range(groups):
        limit = jnp.where(lane // room == u, counts[0, u], limit)
    live = jnp.where(lane % room < limit, dst[...], -1).astype(F32)
    per = width // room
    seat = lax.broadcasted_iota(jnp.int32, (8, width), 1) // room
    for u in range(groups):
        start = u * room // width * width
        row = jnp.broadcast_to(live[:, start : start + width], (8, width))
        turn = lax.rem(e - u + per * groups, per) * room
        row = pltpu.roll(row, turn, 1)
        row = jnp.where(seat == lax.rem(e, per), row, -1.0).astype(BF)
        for target in range(sections):
            msg[target * groups + u, room:, :] = row


def stacked(recv):
    return jnp.concatenate([recv[i, : recv.shape[1] - 8, :] for i in range(recv.shape[0])], axis=0)


def choose(t, sections, act):
    h = lax.axis_index("hist")
    for k in range(sections):

        @pl.when(lax.rem(h - k + sections, sections) == t)
        def _():
            act(k)


def by_target(sources, odt):
    groups, deep, width = sources[0].shape
    room = deep - 8
    per = width // room
    ent_rows = odt.shape[1]
    hots, tables = [], []
    ones = jnp.ones((width, width), BF)
    for g in range(groups // per):
        ids = sources[0][g * per, room:, :].astype(F32)
        for j in range(1, per):
            ids = jnp.maximum(ids, sources[0][g * per + j, room:, :].astype(F32))
        hot = onehot(ids[:1].astype(jnp.int32), ent_rows)
        rows = [
            jnp.concatenate([source[g * per + j, :room, :] for j in range(per)], axis=0)
            for source in sources
        ]
        hots.append(hot)
        tables.append(jnp.concatenate(rows + [ones], axis=1))
        odt[g * width : (g + 1) * width, :] = hot.astype(F32).T.astype(BF)
    hot = jnp.concatenate(hots, axis=1)
    got = dot(hot, jnp.concatenate(tables, axis=0))
    count = len(sources)
    summed = [got[:, m * width : (m + 1) * width] for m in range(count)]
    return hot, summed, 1.0 / jnp.maximum(got[:, count * width :], 1.0)


def through_weight(summed, mates, seat, wnc, first=0):
    total = None
    width = wnc.shape[1]
    for m, part in enumerate(summed, start=first):
        high = part.astype(BF)
        low = (part - high.astype(F32)).astype(BF)
        w = wnc[place(lax.rem(seat - m + mates, mates), width), :]
        out = dot(jnp.concatenate([high, low], axis=1), jnp.concatenate([w, w], axis=0))
        total = out if total is None else total + out
    return total


def index_rows(xt, ent_rows, osr, rid):
    features = xt.shape[1]
    extra = xt[ent_rows:, :].astype(F32).astype(jnp.int32)
    for k in range(osr.shape[1] // features):
        cut = slice(k * features, (k + 1) * features)
        osr[:, cut] = onehot(extra[3 * k : 3 * k + 1], ent_rows)
        ids = extra[3 * k + 1 : 3 * k + 2] * 256 + extra[3 * k + 2 : 3 * k + 3]
        rid[:, cut] = jnp.broadcast_to(ids, (8, features))


def factors(pre_act, gate_open, hidden):
    sig = jax.nn.sigmoid(pre_act)
    new_state = pre_act * sig
    shut = 1.0 - gate_open
    return (
        (new_state - hidden) * gate_open * shut,
        gate_open * (sig * (1.0 + pre_act * (1.0 - sig))),
        shut,
    )


def early_kernel(t, sections, mates, *refs):
    xs = refs[:sections]
    tops, wcat, wnc, bias, odt, osr, rid, hot_out, partial, xt, sem = refs[sections:]
    choose(t, sections, lambda k: pltpu.make_async_copy(xs[k], xt, sem).start())
    ent_rows, width = odt.shape[1], wnc.shape[1]
    h = lax.axis_index("hist")
    hot, summed, scaling = by_target((tops,), odt)
    hot_out[...] = hot
    gathered = through_weight(summed, mates, lax.rem(h, mates), wnc)
    pltpu.make_async_copy(xs[0], xt, sem).wait()
    index_rows(xt, ent_rows, osr, rid)
    straight = dot(xt[:ent_rows, :], wcat[...])
    partial[0] = scaling
    partial[1] = gathered * scaling + straight[:, width:]
    partial[2] = jax.nn.sigmoid(straight[:, :width] + bias[:1, :])
    partial[3] = xt[:ent_rows, place(h, width)].astype(F32)


def state_kernel(t, sections, mates, *refs):
    xs = refs[:sections]
    sources = refs[sections : sections + mates]
    wcat, wnc, bias, coef, odt, osr, rid, xt, sem = refs[sections + mates : sections + mates + 9]
    held, sems = refs[sections + mates + 9 : -1], refs[-1]
    copies = [
        pltpu.make_async_copy(source.at[t], held[m], sems.at[m]) for m, source in enumerate(sources)
    ]
    for copy in copies:
        copy.start()
    choose(t, sections, lambda k: pltpu.make_async_copy(xs[k], xt, sem).start())
    for copy in copies:
        copy.wait()
    ent_rows, width = odt.shape[1], wnc.shape[1]
    h = lax.axis_index("hist")
    _, summed, scaling = by_target(held, odt)
    gathered = through_weight(summed, mates, lax.rem(h, mates), wnc)
    pltpu.make_async_copy(xs[0], xt, sem).wait()
    index_rows(xt, ent_rows, osr, rid)
    straight = dot(xt[:ent_rows, :], wcat[...])
    gate_open = jax.nn.sigmoid(straight[:, :width] + bias[:1, :])
    hidden = xt[:ent_rows, place(h, width)].astype(F32)
    values = factors(gathered * scaling + straight[:, width:], gate_open, hidden)
    for k, value in enumerate((*values, scaling)):
        coef[:, k * width : (k + 1) * width] = value


def query_kernel(qe, qr, qg, wg, ws, wn, bias, top, qp, wcat, wnc, bias_out):
    width = top.shape[1]
    half, mates = wn.shape[1], wn.shape[1] // width
    h = lax.axis_index("hist")
    cols = place(h, width)
    wcat[:, :width] = wg[:, cols]
    wcat[:, width:] = ws[:, cols]
    wnc[...] = wn[h * width // half, :, place(lax.rem(h, mates), width)]
    bias_out[...] = jnp.broadcast_to(bias[:, cols], bias_out.shape)
    grad = qg[:, cols]
    for ids, out in ((qe, top), (qr, qp)):
        hot = onehot(ids[...], out.shape[0]).astype(F32)
        out[...] = lax.dot_general(
            hot,
            grad,
            (((1,), (0,)), ((), ())),
            precision=lax.Precision.HIGHEST,
            preferred_element_type=F32,
        )


def arrived(parts, ret, osr):
    c = parts[0][...]
    for p in parts[1:]:
        c = c + p[...].astype(F32)
    slots, width = osr.shape[1], c.shape[1]
    count = ret.shape[0] // slots
    blocks = [ret[m * slots : (m + 1) * slots, :] for m in range(count)]
    got = dot(osr[...], jnp.concatenate(blocks, axis=1))
    for m in range(count):
        c = c + got[:, m * width : (m + 1) * width]
    return c


def step_kernel(sections, mates, first, *refs):
    h = lax.axis_index("hist")
    if first:
        partial, hot, *mate_rows = refs[1 : 2 + mates]
        c = refs[0][...]
        odt, wcat, wnc, c_out, base, low, rep, bias, *sends = refs[2 + mates :]
        table = jnp.concatenate([stacked(x) for x in mate_rows], axis=1)
        width = wnc.shape[1]
        got = dot(hot[...], table)
        summed = [got[:, m * width : (m + 1) * width] for m in range(mates - 1)]
        scaling = partial[0]
        more = through_weight(summed, mates, lax.rem(h, mates), wnc, first=1)
        al, be, shut = factors(partial[1] + more * scaling, partial[2], partial[3])
    else:
        c = arrived(refs[:sections], refs[sections], refs[sections + 1])
        coef, odt, wcat, wnc, c_out, base, low, rep, bias, *sends = refs[sections + 2 :]
        width = wnc.shape[1]
        al, be, shut, scaling = [coef[:, k * width : (k + 1) * width] for k in range(4)]
    slots = odt.shape[0]
    gate_term = c * al
    pre_term = c * be
    g = (pre_term * scaling).astype(BF)
    out = dot(odt[...], dot(g, wnc[...], WIDE).astype(BF)).astype(BF)
    for m in range(mates):
        rep[m * slots : (m + 1) * slots, :] = out[:, m * width : (m + 1) * width]
    both = jnp.concatenate([gate_term.astype(BF), pre_term.astype(BF)], axis=1)
    outs = []
    for k in range(0, sections, 2):
        rights = [
            wcat[place(lax.rem(h + n, sections), width), :] for n in range(k, min(k + 2, sections))
        ]
        out = dot(both, jnp.concatenate(rights, axis=0), WIDE)
        outs += [out[:, n * width : (n + 1) * width] for n in range(len(rights))]
    for k in range(1, sections):
        sends[k - 1][...] = outs[k].astype(BF)
    low[:, 2 * width :] = g
    low[:, : 2 * width] = both
    c_out[...] = c
    bias[...] = jnp.broadcast_to(jnp.sum(gate_term, axis=0, keepdims=True), bias.shape)
    base[...] = c * shut + outs[0]


def grad_kernel(steps, mates, *refs):
    xs, recv = refs[:steps], refs[steps]
    rest, tops = refs[steps + 1 : steps + mates], refs[steps + mates : steps + 2 * mates - 1]
    refs = refs[steps + 2 * mates - 1 :]
    rel_in = refs[3 * steps : 5 * steps - 2]
    rs_in, gs, ns, bs, rs, held = refs[5 * steps - 2 :]
    h = lax.axis_index("hist")
    for k in range(steps):
        t = steps - 1 - k
        low, bias, odt = refs[3 * k : 3 * k + 3]
        ent_rows = low.shape[0]
        width = low.shape[1] // 3
        seat = lax.rem(h, mates)

        def put(out, at, value):
            out[at] = value if k == 0 else out[at] + value

        held[t] = low[:, : 2 * width]
        put(bs, ..., bias[...])
        replies = dot(odt[...], low[:, 2 * width :]).astype(BF)
        for m in range(mates):
            source = lax.rem(seat - m + mates, mates)
            rows = recv.at[t] if m == 0 else (tops[m - 1] if k == 0 else rest[m - 1].at[t])
            put(ns, place(source, width), dot(stacked(rows), replies, TALL))
    for k in range(steps):
        value = dot(xs[k][:ent_rows, :], held[lax.rem(h - k + steps, steps)], TALL)
        gs[...] = value if k == 0 else gs[...] + value
    rs[...] = rel_sum(steps - 1, rel_in, rs_in[...])


def rel_sum(count, refs, total):
    for t in range(count):
        ret, rid = refs[2 * t : 2 * t + 2]
        slots = rid.shape[1]
        hot = onehot(rid[:1, :], total.shape[0])
        for m in range(ret.shape[0] // slots):
            total = total + dot(hot, ret[m * slots : (m + 1) * slots, :])
    return total


def pack_kernel(sizes, relations, gs, ns, bs, ret, rid, old, mine, other, rs):
    pairs = mine.shape[0]
    width = mine.shape[2]
    core = lax.rem(lax.axis_index("ent"), 2)
    total = rel_sum(1, (ret, rid), old[...])
    level = lax.broadcasted_iota(jnp.int32, total.shape, 0)
    rs[...] = jnp.where(level == relations, bs[:1, :], total)
    pieces = (gs.at[:, :width], gs.at[:, width:], ns, rs)
    for u in range(2 * pairs):
        rows = []
        for piece, size in zip(pieces, sizes):
            deep = piece.shape[0]
            low = min(u * size, deep)
            high = min(low + size, deep)
            if high > low:
                rows.append(piece[low:high, :])
            if high - low < size:
                rows.append(jnp.zeros((size - high + low, width), F32))
        value = jnp.concatenate(rows, axis=0).astype(BF)

        @pl.when(core == u % 2)
        def _():
            mine[u // 2] = value

        @pl.when(core != u % 2)
        def _():
            other[u // 2] = value


def pair_kernel(a, b, out):
    out[...] = (a[...].astype(F32) + b[...].astype(F32)).astype(BF)


def add_kernel(x, out):
    total = x[0].astype(F32)
    for u in range(1, x.shape[0]):
        total = total + x[u].astype(F32)
    for k in range(out.shape[0]):
        out[k] = total.astype(BF)


def pick_kernel(sections, *refs):
    parts = refs[:sections]
    ret, osr = refs[sections : sections + 2]
    saved = refs[sections + 2 : 2 * sections + 1]
    outs = refs[2 * sections + 1 :]
    h = lax.axis_index("hist")
    c = arrived(parts, ret, osr)
    for k in range(sections):
        to = lax.rem(h + k, sections)

        @pl.when(to == 0)
        def _():
            outs[k][...] = c

        for t in range(1, sections):

            @pl.when(to == t)
            def _():
                outs[k][...] = saved[t - 1][...]


def last_kernel(sections, groups, mates, sizes, factor, *refs):
    mine = refs[:sections]
    other = refs[sections : 2 * sections]
    rows = refs[2 * sections : 3 * sections]
    result, neigh, self_, gate, bias, relation, n_all, r_all = refs[3 * sections :]
    width = mine[0].shape[2]
    relations = relation.shape[0]
    h = lax.axis_index("hist")
    core = lax.rem(lax.axis_index("ent"), 2)
    for k in range(sections):
        cols = place(lax.rem(h - k + sections, sections), width)
        result[:, cols] = rows[k][...]
        for z in range(groups // 2):
            for flip, piece in enumerate((mine[k], other[k])):
                u = 2 * z + (core if flip == 0 else 1 - core)
                at = 0
                for out, size in zip((gate, self_, n_all, r_all), sizes):
                    out[place(u, size), cols] = piece[z, at : at + size, :].astype(F32) * factor
                    at += size
    relation[...] = r_all[:relations, :]
    bias[...] = r_all[relations : relations + 1, :]
    half = neigh.shape[1]
    for f in range(sections):
        neigh[f // mates, :, f % mates * width : (f % mates + 1) * width] = n_all[
            :half, f * width : (f + 1) * width
        ]


def on_device(
    states,
    w_neigh,
    w_self,
    w_gate,
    b_gate,
    relation,
    edge_src,
    edge_rel,
    edge_dst,
    send_counts,
    query_ent,
    query_rel,
    query_grad,
):
    groups = lax.axis_size("ent")
    sections = lax.axis_size("hist")
    ent_rows, features = states.shape[1:]
    slots = edge_src.shape[1]
    room = slots // groups
    width = features // sections
    blocks, half = w_neigh.shape[:2]
    mates = sections // blocks
    relations = relation.shape[0]
    hidden = far(states[0])
    relation, edge_src, edge_rel, edge_dst = map(far, (relation, edge_src, edge_rel, edge_dst))
    bias_row = b_gate.reshape(1, features)
    smem = pl.BlockSpec(memory_space=pltpu.SMEM)
    members = mates * groups
    block_groups = [list(range(b * members, (b + 1) * members)) for b in range(blocks)]

    def turn(x, k):
        return lax.ppermute(x, "hist", [(i, (i + k) % sections) for i in range(sections)])

    def to_mate(x, m):
        route = [(i, i // mates * mates + (i + m) % mates) for i in range(sections)]
        return lax.ppermute(x, "hist", route)

    def to_core(x):
        return lax.ppermute(x, "ent", [(i, i ^ 1) for i in range(groups)])

    rows_f32 = sds((ent_rows, width), F32)
    rows_bf = sds((ent_rows, width), BF)
    last = sections - 1

    ins = (hidden, edge_src, edge_rel)
    (xp,) = run(pre_kernel, ins, [whole(x) for x in ins], [far(sds((ent_rows + 8, features), BF))])
    turned = [turn(raw(xp), k) for k in range(1, sections)]
    xs = [xp] + [far(x) for x in turned]
    (msg,) = run(
        functools.partial(send_kernel, sections, groups),
        (hidden, relation, edge_src, edge_dst, edge_rel, send_counts),
        [whole(hidden), whole(relation)] + [whole(edge_src)] * 3 + [smem],
        [far(sds((sections * groups, room + 8, width), BF))],
    )
    recv = lax.all_to_all(
        raw(msg), ("hist", "ent"), split_axis=0, concat_axis=0, tiled=True
    ).reshape(sections, groups, room + 8, width)

    rel_rows = round_up(relations + 1, 8)
    qe = query_ent.reshape(1, -1)
    qr = query_rel.reshape(1, -1)
    ins = tuple(map(far, (qe, qr, query_grad, w_gate, w_self, w_neigh, bias_row)))
    top, rs, wcat, wnc, bias_cols = run(
        query_kernel,
        ins,
        [whole(x) for x in ins],
        [
            far(x)
            for x in (
                rows_f32,
                sds((rel_rows, width), F32),
                sds((features, 2 * width), BF),
                sds((half, width), BF),
                sds((8, width), F32),
            )
        ],
    )
    recv, held = lax.optimization_barrier((recv, raw(wnc)))
    wnc = far(held)
    tops, rest = recv[last], recv[:last]
    mate_tops = [to_mate(tops, m) for m in range(1, mates)]
    rest, *mate_tops = lax.optimization_barrier((rest, *mate_tops))
    mate_rest = [to_mate(rest, m) for m in range(1, mates)]
    any_space = pl.BlockSpec(memory_space=pl.ANY)

    shapes = [
        far(x)
        for x in (
            sds((slots, ent_rows), BF),
            sds((ent_rows, slots), BF),
            sds((8, slots), jnp.int32),
        )
    ]
    row_scratch = [pltpu.VMEM((ent_rows + 8, features), BF), pltpu.SemaphoreType.DMA]

    def prepare_first():
        ins = (xp, *turned, tops, wcat, wnc, bias_cols)
        return run(
            functools.partial(early_kernel, last, sections, mates),
            ins,
            [any_space] * sections + [whole(x) for x in ins[sections:]],
            shapes + [sds((ent_rows, slots), BF), sds((4, ent_rows, width), F32)],
            row_scratch,
        )

    def prepare(t):
        ins = (*xs, far(recv), *map(far, mate_rest), wcat, wnc, bias_cols)
        return run(
            functools.partial(state_kernel, t, sections, mates),
            ins,
            [any_space] * (sections + mates) + [whole(x) for x in ins[sections + mates :]],
            [far(sds((ent_rows, 4 * width), F32))] + shapes,
            row_scratch
            + [pltpu.VMEM(tops.shape, BF)] * mates
            + [pltpu.SemaphoreType.DMA((mates,))],
        )

    saved = [None] * (sections + 1)
    grad_ins = [*xs, far(recv), *map(far, mate_rest), *map(far, mate_tops)]
    rel_ins = []
    for t in range(last, -1, -1):
        if t == last:
            odt, osr, rid, hot, partial = prepare_first()
            ins = (top, partial, hot, *mate_tops, odt, wcat, wnc)
        else:
            coef, odt, osr, rid = prepare(t)
            ins = (*parts, ret, osr_before, coef, odt, wcat, wnc)
        c, base, low, rep, bias, *sends = run(
            functools.partial(step_kernel, sections, mates, t == last),
            ins,
            [whole(x) for x in ins],
            [
                far(x)
                for x in (
                    rows_f32,
                    rows_f32,
                    sds((ent_rows, 3 * width), BF),
                    sds((mates * slots, width), BF),
                    sds((8, width), F32),
                    *[rows_bf] * (sections - 1),
                )
            ],
        )
        if t == last:
            sent, *mate_rest = lax.optimization_barrier((raw(sends[0]), *mate_rest))
            sends[0] = far(sent)
        saved[t + 1] = c
        ret = lax.all_to_all(
            raw(rep).reshape(members, room, width),
            ("hist", "ent"),
            split_axis=0,
            concat_axis=0,
            tiled=True,
            axis_index_groups=block_groups,
        ).reshape(mates * slots, width)
        parts = [base] + [turn(raw(x), k + 1) for k, x in enumerate(sends)]
        osr_before = osr
        grad_ins += [low, bias, odt]
        rel_ins += [far(ret), rid]

    grad_ins += [*rel_ins[:-2], rs]
    gs, ns, bs, rs = run(
        functools.partial(grad_kernel, sections, mates),
        grad_ins,
        [whole(x) for x in grad_ins],
        [far(sds((features, 2 * width), F32)), far(sds((half, width), F32)), far(sds((8, width), F32)), far(sds((rel_rows, width), F32))],
        [pltpu.VMEM((sections, ent_rows, 2 * width), BF)],
    )
    ret, *moved = lax.optimization_barrier((ret, *parts[1:]))
    parts = [parts[0], *moved]
    ins = (*parts, ret, osr_before, *saved[1:sections])
    picks = run(
        functools.partial(pick_kernel, sections),
        ins,
        [whole(x) for x in ins],
        [rows_f32] * sections,
    )
    home = [picks[0]] + [turn(picks[k], k) for k in range(1, sections)]
    sizes = tuple(
        round_up(-(-rows // groups), 16) for rows in (features, features, half, rel_rows)
    )
    chunk = sum(sizes)
    pairs = groups // 2
    ins = (gs, ns, bs, ret, rid, rs)
    ins = tuple(ins)
    mine, other = run(
        functools.partial(pack_kernel, sizes, relations),
        ins,
        [whole(x) for x in ins],
        [sds((pairs, chunk, width), BF)] * 2,
        [pltpu.VMEM((rel_rows, width), F32)],
    )
    ins = (mine, to_core(other))
    (landed,) = run(pair_kernel, ins, [whole(x) for x in ins], [sds((pairs, chunk, width), BF)])
    same = [[i for i in range(groups) if i % 2 == core] for core in range(2)]

    def a2a_same(x):
        return lax.all_to_all(
            x, "ent", split_axis=0, concat_axis=0, tiled=True, axis_index_groups=same
        )

    landed, *home = lax.optimization_barrier((a2a_same(landed), *home))
    (copies,) = run(add_kernel, (landed,), [whole(landed)], [sds((pairs, chunk, width), BF)])
    column = a2a_same(copies)
    mine = [column] + [turn(column, k) for k in range(1, sections)]
    other = [to_core(x) for x in mine]
    ins = (*mine, *other, *home)
    factor = 1.0 / math.sqrt(sections * ent_rows * groups)
    tall = [size * groups for size in sizes]
    result, neigh, self_, gate, bias, rel = pl.pallas_call(
        functools.partial(last_kernel, sections, groups, mates, sizes, factor),
        name="last",
        compiler_params=pltpu.CompilerParams(vmem_limit_bytes=24 << 20),
        grid=(1,),
        in_specs=[whole(x) for x in ins],
        out_specs=[
            block((ent_rows, features)),
            block(w_neigh.shape),
            block((tall[1], features)),
            block((tall[0], features)),
            block((1, features)),
            block((relations, features)),
        ],
        out_shape=[
            sds((ent_rows, features), F32),
            sds(w_neigh.shape, F32),
            sds((tall[1], features), F32),
            sds((tall[0], features), F32),
            sds((1, features), F32),
            sds((relations, features), F32),
        ],
        scratch_shapes=[
            pltpu.VMEM((tall[2], features), F32),
            pltpu.VMEM((tall[3], features), F32),
        ],
    )(*ins)
    return (
        result[None],
        neigh,
        self_[:features],
        gate[:features],
        bias.reshape(features),
        rel,
    )


def solution(mesh):
    return jax.shard_map(
        on_device,
        mesh=mesh,
        in_specs=(
            P("hist", "ent", None),
            P(),
            P(),
            P(),
            P(),
            P(),
            P("hist", "ent"),
            P("hist", "ent"),
            P("hist", "ent"),
            P("hist", "ent"),
            P("ent"),
            P("ent"),
            P("ent", None),
        ),
        out_specs=(P("hist", "ent", None), P(), P(), P(), P(), P()),
        check_vma=False,
    )
```
